512 devices in a mesh: freq: 16 (over y, core), offset: 32 (over x, z).
Axes of the slice: x: 4, y: 8, z: 8, core: 2. Of those that a mesh axis runs over, the one named last changes fastest.
Arguments:
- raw_traces: bfloat16 [32768, 2048], P('offset', 'freq'), may hold values from -6 to 6
- trace_slot: int32 [32, 1024], P(None, 'offset'), may hold values from 0 to 1023, as said below
- offset_index: int32 [1024], replicated, may hold values from 1 to 1023
- slowness_index: int32 [256], replicated, may hold values from 0 to 511
Outputs:
- radon: float32 [256, 1024, 64], P('offset', 'freq')
The draws below stay inside these ranges and needn't reach their ends.
Inputs may be any that keep to these rules, and one draw needn't show every extreme that they name: `trace_slot`: in every aligned block of 32 columns, the 32 x 32 entries name each of 0 to 1023 exactly once.
All inputs are finite; a program needn't handle non-finite values.
Results may differ from the reference program's by a relative error of at most 0.0046.
Values may be sent and summed in bfloat16 or wider, within the bound.
A program may use at most 64 MiB of HBM per device.

```python
import math
import jax
import jax.numpy as jnp
from jax import lax

NT = 2048
NF = 1024
NP = 256
GATHERS = 32
H_DEV = 32
NH = 1024
N_OFFSET = 32


def draw_trace_slot(key, part):
    block_rows = GATHERS * H_DEV
    key_list = jax.random.split(jax.random.fold_in(key, 7), N_OFFSET)
    orders = jax.vmap(lambda single: jax.random.permutation(single, block_rows))(key_list)
    shaped = orders.reshape(N_OFFSET, GATHERS, H_DEV)
    return jnp.transpose(shaped, (1, 0, 2)).reshape(GATHERS, N_OFFSET * H_DEV).astype(jnp.int32)


def place_ends(drawn, stream_key, low, largest):
    place = [jax.random.randint(jax.random.fold_in(stream_key, axis), (), 0, length) for axis, length in enumerate(drawn.shape)]
    longest = drawn.shape.index(max(drawn.shape))
    beside = place[:longest] + [(place[longest] + 1) % drawn.shape[longest]] + place[longest + 1:]
    return drawn.at[tuple(place)].set(low).at[tuple(beside)].set(largest)


def shard_levels(stream_key, extent, cuts, smallest, top_value):
    factor_of, own = 1.0, jax.random.fold_in(stream_key, 6)
    for dim, parts in cuts:
        steps = jnp.exp(jax.random.uniform(jax.random.fold_in(own, dim), (parts,), jnp.float32, smallest / len(cuts), top_value / len(cuts)))
        factor_of = factor_of * jnp.repeat(steps, extent[dim] // parts).reshape([-1 if axis == dim else 1 for axis in range(len(extent))])
    return factor_of


def scatter_about(own_key, shape, scale, limit, cuts=(), kind=jnp.bfloat16):
    gain = shard_levels(own_key, shape, cuts, -0.22, 0.18) if cuts else 1.0
    result = jax.random.normal(own_key, shape, jnp.float32) * scale * gain
    return jnp.minimum(jnp.maximum(result, -limit), limit).astype(kind)


def setup_inputs(seed: int = 0) -> dict:
    streams_of = jax.random.split(jax.random.key(seed), 5)
    raw_traces = scatter_about(streams_of[0], (GATHERS * NH, NT), 1.0, 6.0, ((0, 32), (1, 16)))
    trace_slot = draw_trace_slot(jax.random.fold_in(streams_of[4], 71), 0)
    offset_index = place_ends(jax.random.randint(streams_of[2], (NH,), 1, 1024), jax.random.fold_in(streams_of[2], 1), 1, 1023).astype(jnp.int32)
    slowness_index = place_ends(jax.random.randint(streams_of[3], (NP,), 0, 512), jax.random.fold_in(streams_of[3], 1), 0, 511).astype(jnp.int32)
    return {"raw_traces": raw_traces, "trace_slot": trace_slot, "offset_index": offset_index, "slowness_index": slowness_index}


APEX_TIME = 100.0
CURVATURE = 0.0003

def moveout(slowness, offset_grid):
    spread = CURVATURE * slowness.astype(jnp.float32)[:, None] * offset_grid.astype(jnp.float32)[None, :]
    return jnp.sqrt(APEX_TIME * APEX_TIME + spread * spread) - APEX_TIME

def reference(raw_traces, trace_slot, offset_index, slowness_index):
    block_rows = GATHERS * H_DEV
    row_base = jnp.arange(NH, dtype=jnp.int32) // H_DEV * block_rows
    trace_rows = (trace_slot + row_base[None, :]).reshape(-1).astype(jnp.int32)
    gathered = raw_traces[trace_rows].astype(jnp.float32)
    sample_ids = jnp.arange(NT, dtype=jnp.int32)[:, None]
    freq_ids = jnp.arange(NF, dtype=jnp.int32)[None, :]
    turn_ids = sample_ids * (2 * freq_ids + 1) % (2 * NT)
    angles = turn_ids.astype(jnp.float32) * (math.pi / NT)
    fourier_table = (jnp.concatenate([jnp.cos(angles), -jnp.sin(angles)], axis=1) / math.sqrt(NT)).astype(jnp.bfloat16)
    spectrum = jnp.dot(gathered, fourier_table.astype(jnp.float32), preferred_element_type=jnp.float32, precision=lax.Precision.HIGHEST).astype(jnp.bfloat16)
    spectrum = spectrum.reshape(GATHERS, NH, 2 * NF)
    real_all = jnp.transpose(spectrum[:, :, :NF], (2, 1, 0))
    imag_all = jnp.transpose(spectrum[:, :, NF:], (2, 1, 0))
    delays = moveout(slowness_index, offset_index)

    def one_frequency(inputs):
        freq_one, real_in, imag_in = inputs
        angular = (2 * freq_one + 1).astype(jnp.float32) * (math.pi / NT)
        phases = angular * delays
        cosine = jnp.cos(phases).astype(jnp.bfloat16).astype(jnp.float32)
        sines = jnp.sin(phases).astype(jnp.bfloat16).astype(jnp.float32)
        real_data = real_in.astype(jnp.float32)
        imag_data = imag_in.astype(jnp.float32)
        high = lax.Precision.HIGHEST
        real_out = jnp.dot(cosine, real_data, precision=high) - jnp.dot(sines, imag_data, precision=high)
        imag_out = jnp.dot(sines, real_data, precision=high) + jnp.dot(cosine, imag_data, precision=high)
        return jnp.concatenate([real_out, imag_out], axis=1)
    panel = lax.map(one_frequency, (jnp.arange(NF, dtype=jnp.int32), real_all, imag_all))
    return jnp.transpose(panel, (1, 0, 2)) * (1.0 / math.sqrt(NH))
```

```python
import math

import jax
import jax.numpy as jnp
from jax import lax
from jax.sharding import Mesh
from jax.sharding import PartitionSpec as P

NF = 1024
OFFSET = ("offset_0", "offset_1")
APEX_TIME = 100.0
CURVATURE = 0.0003


def moveout(slowness, offset_grid):
    spread = (
        CURVATURE * slowness.astype(jnp.float32)[:, None] * offset_grid.astype(jnp.float32)[None, :]
    )
    return jnp.sqrt(APEX_TIME * APEX_TIME + spread * spread) - APEX_TIME


def whole_table(total_time):
    column_total = 2 * NF
    column = jnp.arange(column_total, dtype=jnp.int32)
    freq_ids = column // 2
    shifts = jnp.where(column % 2 == 0, 0, total_time // 2).astype(jnp.int32)
    odd_rates = 2 * freq_ids + 1
    fine_size = 64
    coarse_size = total_time // fine_size
    period = 2 * total_time
    coarse_ids = jnp.arange(coarse_size, dtype=jnp.int32)[:, None]
    fine_ids = jnp.arange(fine_size, dtype=jnp.int32)[:, None]
    coarse_turn = coarse_ids * fine_size % period * odd_rates[None, :] % period
    fine_turn = (fine_ids * odd_rates[None, :] + shifts[None, :]) % period
    coarse_angle = coarse_turn.astype(jnp.float32) * (math.pi / total_time)
    fine_angle = fine_turn.astype(jnp.float32) * (math.pi / total_time)
    coarse_cos = jnp.cos(coarse_angle)
    coarse_sin = jnp.sin(coarse_angle)
    fine_cos = jnp.cos(fine_angle)
    fine_sin = jnp.sin(fine_angle)
    values = (
        coarse_cos[:, None, :] * fine_cos[None, :, :]
        - coarse_sin[:, None, :] * fine_sin[None, :, :]
    )
    values = values.reshape(total_time, column_total)
    return (values * (1.0 / math.sqrt(total_time))).astype(jnp.bfloat16)


def local(raw_traces, trace_slot, offset_index, slowness_index):
    gathers, local_offsets = trace_slot.shape
    local_times = raw_traces.shape[1]
    nk = lax.axis_size("freq")
    no = lax.axis_size(OFFSET)
    total_time = local_times * nk
    band = NF // nk
    pair = band // no
    hs = local_offsets // nk
    rows = hs * gathers
    picked = raw_traces[trace_slot.T.reshape(-1)]
    grouped = picked.reshape(nk, rows, local_times)
    table = whole_table(total_time)
    series = lax.all_to_all(grouped, "freq", split_axis=0, concat_axis=2, tiled=True)
    series = series.reshape(rows, total_time)
    spectrum = jnp.dot(series, table, preferred_element_type=jnp.float32).astype(jnp.bfloat16)
    c = 2 * pair
    spectrum = spectrum.reshape(hs, gathers, nk, no, c)
    spectrum = jnp.transpose(spectrum, (2, 3, 0, 4, 1)).reshape(nk, no, hs, c * gathers)
    first = lax.all_to_all(spectrum, "freq", split_axis=0, concat_axis=0, tiled=True)
    first = jnp.transpose(first, (1, 0, 2, 3)).reshape(no, nk * hs, c * gathers)
    second = lax.all_to_all(first, OFFSET, split_axis=0, concat_axis=0, tiled=True)
    spectra = second.reshape(no * nk * hs, c * gathers)

    freq_ids = lax.axis_index("freq") * band + lax.axis_index(OFFSET) * pair + jnp.arange(pair, dtype=jnp.int32)
    angular = (2 * freq_ids + 1).astype(jnp.float32) * (math.pi / total_time)
    delays = moveout(slowness_index, offset_index)
    phases = angular[:, None, None] * delays[None, :, :]
    cosine = jnp.cos(phases).astype(jnp.bfloat16)
    sines = jnp.sin(phases).astype(jnp.bfloat16)
    scale = 1.0 / math.sqrt(local_offsets * no)
    panels = []
    for f in range(pair):
        data = spectra[:, f * 2 * gathers:(f + 1) * 2 * gathers]
        cd = jnp.dot(cosine[f], data, preferred_element_type=jnp.float32)
        sd = jnp.dot(sines[f], data, preferred_element_type=jnp.float32)
        real_out = cd[:, :gathers] - sd[:, gathers:]
        imag_out = sd[:, :gathers] + cd[:, gathers:]
        panels.append(jnp.concatenate([real_out, imag_out], axis=1))
    panel = jnp.concatenate(panels, axis=1) * scale
    nps = panel.shape[0] // no
    panel = panel.reshape(no, nps, pair * 2 * gathers)
    got = lax.all_to_all(panel, OFFSET, split_axis=0, concat_axis=0, tiled=True)
    got = got.reshape(no, nps, pair, 2 * gathers)
    return jnp.transpose(got, (1, 0, 2, 3)).reshape(nps, band, 2 * gathers)


def solution(mesh):
    torus = Mesh(mesh.devices.reshape(mesh.shape["freq"], 4, 8), ("freq", "offset_0", "offset_1"))
    placed = (P(OFFSET, "freq"), P(None, OFFSET), P(), P())
    return jax.shard_map(
        local, mesh=torus, in_specs=placed, out_specs=P(OFFSET, "freq", None), check_vma=False
    )
```

```python
import functools
import math

import jax
import jax.numpy as jnp
import numpy as np
from jax import lax
from jax.experimental import pallas as pl
from jax.experimental.pallas import tpu as pltpu
from jax.sharding import PartitionSpec as P

NT = 2048
NF = 1024
NP = 256
G = 32
HB = 32
NH = 1024
NK = 16
NO = 32
NX = 4
NZ = 8
APEX_TIME = 100.0
CURVATURE = 0.0003
MESH = pl.DeviceIdType.MESH
F32 = jnp.float32
BF16 = jnp.bfloat16


def dft_tables():
    n = np.arange(256)[None, :]
    a = np.arange(128)[:, None]
    t0 = 2 * np.pi * ((a * n) % 256) / 256
    t1 = 2 * np.pi * (((255 - a) * n) % 256) / 256
    rows = [
        np.concatenate([np.cos(t0), np.sin(t0)], 1),
        np.concatenate([-np.sin(t0), np.cos(t0)], 1),
        np.concatenate([np.cos(t1), np.sin(t1)], 1),
        np.concatenate([np.sin(t1), -np.cos(t1)], 1),
    ]
    table = np.concatenate(rows, 0)
    m = 2 * np.arange(4)[:, None] + 1
    turn = np.pi * (m * n) / 2048
    twiddle = np.concatenate([np.cos(turn), np.sin(turn)], 0) / math.sqrt(NT)
    return table.astype(np.float32), twiddle.astype(np.float32)


def half_turn_fit(odd, terms):
    nodes = 0.25 * (np.cos(np.pi * (np.arange(400) + 0.5) / 400) + 1) / 2
    r = np.sqrt(nodes)
    want = np.sin(np.pi * r) / r if odd else np.cos(np.pi * r)
    fit = np.polynomial.chebyshev.Chebyshev.fit(nodes, want, terms - 1, domain=[0, 0.25])
    return [float(v) for v in fit.convert(kind=np.polynomial.Polynomial).coef]


SIN_FIT = half_turn_fit(True, 6)
COS_FIT = half_turn_fit(False, 6)


def horner(x, coef):
    total = coef[-1] * x + coef[-2]
    for value in coef[-3::-1]:
        total = total * x + value
    return total


def far_first(i, n):
    half = n // 2
    return half + ((i + 1) // 2) * (1 - 2 * (i % 2))


def kernel(raw, slot, offs, slow, twid, table_hbm, out,
           table, send_a, recv_a, spec, send_b, recv_b, wide, send_c, recv_c, weights, curve,
           send_d, recv_d,
           ssem_a, rsem_a, ssem_b, rsem_b, ssem_c, rsem_c, ssem_d, rsem_d, table_sem):
    me_k = lax.axis_index("freq")
    me_o = lax.axis_index("offset")
    me_x, me_z = me_o // NZ, me_o % NZ

    def peer_k(i):
        return (me_k + far_first(i, NK)) % NK

    def peer_o(i):
        dz = far_first(i // NX, NZ)
        dx = far_first(i % NX, NX)
        return ((me_x + dx) % NX) * NZ + (me_z + dz) % NZ

    barrier = pltpu.get_barrier_semaphore()

    def greet_k(i, c):
        pl.semaphore_signal(barrier, inc=1, device_id=(peer_k(i), me_o), device_id_type=MESH)
        return c

    def greet_o(i, c):
        pl.semaphore_signal(barrier, inc=1, device_id=(me_k, peer_o(i)), device_id_type=MESH)
        return c

    lax.fori_loop(0, NO - 1, greet_o, 0)
    lax.fori_loop(0, NK - 1, greet_k, 0)
    table_copy = pltpu.make_async_copy(table_hbm, table, table_sem)
    table_copy.start()

    lane_ids = lax.broadcasted_iota(jnp.int32, (G, HB * G), 1)
    data = raw[...]
    for kk in range(NK):
        picks = [
            jnp.where(slot[:, 2 * kk + h:2 * kk + h + 1] == lane_ids, 1.0, 0.0) for h in range(2)
        ]
        chosen = jnp.concatenate(picks, axis=0).astype(BF16)
        send_a[kk] = jnp.dot(chosen, data, preferred_element_type=F32).astype(BF16)

    pl.semaphore_wait(barrier, NO - 1 + NK - 1)

    def copy_k(src, dst, ssem, rsem, there, here):
        return pltpu.make_async_remote_copy(
            src_ref=src.at[there], dst_ref=dst.at[here], send_sem=ssem.at[there],
            recv_sem=rsem.at[here], device_id=(there, me_o), device_id_type=MESH)

    def copy_o(src, dst, ssem, rsem, there, here):
        return pltpu.make_async_remote_copy(
            src_ref=src.at[there], dst_ref=dst.at[here], send_sem=ssem.at[there],
            recv_sem=rsem.at[here], device_id=(me_k, there), device_id_type=MESH)

    def start_all(make, count, peer, me, *refs):
        def step(i, c):
            make(*refs, peer(i), me).start()
            return c
        lax.fori_loop(0, count, step, 0)

    def await_recv(make, count, peer, *refs):
        def step(i, c):
            make(*refs, peer(i), peer(i)).wait_recv()
            return c
        lax.fori_loop(0, count, step, 0)

    def await_send(make, count, peer, me, *refs):
        def step(i, c):
            make(*refs, peer(i), me).wait_send()
            return c
        lax.fori_loop(0, count, step, 0)

    a_refs = (send_a, recv_a, ssem_a, rsem_a)
    b_refs = (send_b, recv_b, ssem_b, rsem_b)
    c_refs = (send_c, recv_c, ssem_c, rsem_c)
    d_refs = (send_d, recv_d, ssem_d, rsem_d)

    start_all(copy_k, NK - 1, peer_k, me_k, *a_refs)
    recv_a[me_k] = send_a[me_k]

    for half in range(2):
        row = slow[:, 128 * half:128 * half + 128].astype(F32) * CURVATURE
        curve[128 * half:128 * half + 128, :] = jnp.transpose(jnp.broadcast_to(row, (128, 128)))
    first = 64 * me_k + 8 * me_z + me_x
    second = 64 * me_k + 8 * me_z + 7 - me_x
    rates = [(2 * f + 1).astype(F32) * (1.0 / (2 * NT)) for f in (first, second)]

    def weigh(block, c):
        rows = pl.ds(pl.multiple_of(block * 16, 16), 16)
        low = pl.ds(pl.multiple_of(block * 16 + NP, 16), 16)
        steep = curve[rows, :]
        for part in range(NH // 256):
            lanes = slice(256 * part, 256 * part + 256)
            spread = jnp.concatenate([steep, steep], axis=1) * offs[:, lanes].astype(F32)
            delay = jnp.sqrt(APEX_TIME * APEX_TIME + spread * spread) - APEX_TIME
            for f in range(2):
                turns = delay * rates[f]
                r = turns - jnp.round(turns)
                r2 = r * r
                s = horner(r2, SIN_FIT) * r
                q = horner(r2, COS_FIT)
                weights[f, rows, lanes] = (1.0 - 2.0 * (s * s)).astype(BF16)
                weights[f, low, lanes] = (2.0 * (s * q)).astype(BF16)
        return c

    lax.fori_loop(0, NP // 16, weigh, 0)

    await_recv(copy_k, NK - 1, peer_k, *a_refs)

    x = [jnp.concatenate([recv_a[2 * d], recv_a[2 * d + 1]], axis=1).astype(F32) for d in range(8)]
    less = [x[d] - x[8 - d] for d in range(1, 4)]
    more = [x[d] + x[8 - d] for d in range(1, 4)]
    for b in range(4):
        m = 2 * b + 1
        yr = x[0]
        yi = x[4] * (-math.sin(math.pi * m / 2))
        for d in range(1, 4):
            yr = yr + less[d - 1] * math.cos(math.pi * d * m / 8)
            yi = yi - more[d - 1] * math.sin(math.pi * d * m / 8)
        tc = twid[b:b + 1, :]
        ts = twid[4 + b:5 + b, :]
        spec[64 * b:64 * b + 64, 0:256] = (yr * tc + yi * ts).astype(BF16)
        spec[64 * b:64 * b + 64, 256:512] = (yi * tc - yr * ts).astype(BF16)
    table_copy.wait()
    lane = lax.broadcasted_iota(jnp.int32, (128, 128), 1) // 32
    spec_all = spec[...]
    parts = [
        lax.dot_general(table[128 * c:128 * c + 128, :], spec_all, (((1,), (1,)), ((), ())),
                        preferred_element_type=F32)
        for c in range(4)
    ]
    for tile in range(2):
        pieces = [p[:, 128 * tile:128 * tile + 128] for p in parts]
        for h in range(2):
            both = []
            for b in range(2):
                i = 2 * b + h
                total = pieces[0] if i == 0 else pltpu.roll(pieces[0], (0 - i) * 32 % 128, 1)
                for c in range(1, 4):
                    moved = pieces[c] if c == i else pltpu.roll(pieces[c], (c - i) * 32 % 128, 1)
                    total = jnp.where(lane == c, moved, total)
                both.append(total.reshape(NK, 8, 128))
            rows = slice(32 * h + 16 * tile, 32 * h + 16 * tile + 16)
            send_b[:, rows, :] = jnp.concatenate(both, axis=1).astype(BF16)

    start_all(copy_k, NK - 1, peer_k, me_k, *b_refs)
    recv_b[me_k] = send_b[me_k]
    await_recv(copy_k, NK - 1, peer_k, *b_refs)

    wide[...] = recv_b[...].astype(F32).reshape(NK * 64, 128)
    for q in range(NO):
        send_c[q] = wide[pl.ds(q, 32, stride=32), :].astype(BF16)
    start_all(copy_o, NO - 1, peer_o, me_o, *c_refs)
    recv_c[me_o] = send_c[me_o]
    await_recv(copy_o, NO - 1, peer_o, *c_refs)

    spectra = recv_c[...].reshape(NH, 128)
    lane = lax.broadcasted_iota(jnp.int32, (64, 128), 1)
    for block in range(NP // 64):
        rows = slice(64 * block, 64 * block + 64)
        low = slice(NP + 64 * block, NP + 64 * block + 64)
        cosine = [jnp.dot(weights[f, rows, :], spectra, preferred_element_type=F32) for f in range(2)]
        sines = [jnp.dot(weights[f, low, :], spectra, preferred_element_type=F32) for f in range(2)]
        ca = jnp.where(lane < 64, cosine[0], cosine[1])
        sa = jnp.where(lane < 64, sines[0], sines[1])
        swapped = jnp.where(lane % 64 < 32, -pltpu.roll(sa, 96, 1), pltpu.roll(sa, 32, 1))
        panel = (ca + swapped) * (1.0 / math.sqrt(NH))
        send_d[8 * block:8 * block + 8] = panel.reshape(8, 8, 128)

    start_all(copy_o, NO - 1, peer_o, me_o, *d_refs)
    recv_d[me_o] = send_d[me_o]
    await_recv(copy_o, NO - 1, peer_o, *d_refs)
    for o in range(NO):
        one = recv_d[o]
        f0 = 8 * (o % NZ) + o // NZ
        f1 = 8 * (o % NZ) + 7 - o // NZ
        out[pl.ds(f0, 8, stride=64), :] = one[:, 0:64]
        out[pl.ds(f1, 8, stride=64), :] = one[:, 64:128]

    await_send(copy_k, NK - 1, peer_k, me_k, *a_refs)
    await_send(copy_k, NK - 1, peer_k, me_k, *b_refs)
    await_send(copy_o, NO - 1, peer_o, me_o, *c_refs)
    await_send(copy_o, NO - 1, peer_o, me_o, *d_refs)


def local(raw_traces, trace_slot, offset_index, slowness_index):
    table, twiddle = dft_tables()
    vmem = pl.BlockSpec(memory_space=pltpu.VMEM)
    dma = pltpu.SemaphoreType.DMA
    got = pl.pallas_call(
        kernel,
        out_shape=jax.ShapeDtypeStruct((8 * 64, 64), F32),
        in_specs=[vmem] * 5 + [pl.BlockSpec(memory_space=pl.ANY)],
        out_specs=vmem,
        scratch_shapes=[
            pltpu.VMEM((512, 512), BF16),
            pltpu.VMEM((NK, 64, 128), BF16), pltpu.VMEM((NK, 64, 128), BF16),
            pltpu.VMEM((256, 512), BF16),
            pltpu.VMEM((NK, 64, 128), BF16), pltpu.VMEM((NK, 64, 128), BF16),
            pltpu.VMEM((NK * 64, 128), F32),
            pltpu.VMEM((NO, 32, 128), BF16), pltpu.VMEM((NO, 32, 128), BF16),
            pltpu.VMEM((2, 2 * NP, NH), BF16),
            pltpu.VMEM((NP, 128), F32),
            pltpu.VMEM((NO, 8, 128), F32), pltpu.VMEM((NO, 8, 128), F32),
            dma((NK,)), dma((NK,)), dma((NK,)), dma((NK,)),
            dma((NO,)), dma((NO,)), dma((NO,)), dma((NO,)), dma(()),
        ],
        compiler_params=pltpu.CompilerParams(
            collective_id=0, has_side_effects=True, vmem_limit_bytes=32 * 1024 * 1024),
        name="radon",
    )(raw_traces, trace_slot, offset_index.reshape(1, NH), slowness_index.reshape(1, NP),
      jnp.asarray(twiddle), jnp.asarray(table, dtype=BF16))
    return got.reshape(8, 64, 64)


def solution(mesh):
    placed = (P("offset", "freq"), P(None, "offset"), P(), P())
    return jax.shard_map(
        local, mesh=mesh, in_specs=placed, out_specs=P("offset", "freq", None), check_vma=False
    )
```

```python
import functools
import math

import jax
import jax.numpy as jnp
import numpy as np
from jax import lax
from jax.experimental import pallas as pl
from jax.experimental.pallas import tpu as pltpu
from jax.sharding import PartitionSpec as P

NT = 2048
NF = 1024
NP = 256
G = 32
HB = 32
NH = 1024
NK = 16
NO = 32
NX = 4
NZ = 8
APEX_TIME = 100.0
CURVATURE = 0.0003
MESH = pl.DeviceIdType.MESH
F32 = jnp.float32
BF16 = jnp.bfloat16


def dft_tables():
    n = np.arange(256)[None, :]
    row = np.arange(128)
    a = (row % NK * NZ + row // NK)[:, None]
    t0 = 2 * np.pi * ((a * n) % 256) / 256
    t1 = 2 * np.pi * (((255 - a) * n) % 256) / 256
    rows = [
        np.concatenate([np.cos(t0), np.sin(t0)], 1),
        np.concatenate([-np.sin(t0), np.cos(t0)], 1),
        np.concatenate([np.cos(t1), np.sin(t1)], 1),
        np.concatenate([np.sin(t1), -np.cos(t1)], 1),
    ]
    table = np.concatenate(rows, 0)
    m = 2 * np.arange(4)[:, None] + 1
    turn = np.pi * (m * n) / 2048
    twiddle = np.concatenate([np.cos(turn), np.sin(turn)], 0) / math.sqrt(NT)
    return table.astype(np.float32), twiddle.astype(np.float32)


def half_turn_fit(odd, terms):
    nodes = 0.25 * (np.cos(np.pi * (np.arange(400) + 0.5) / 400) + 1) / 2
    r = np.sqrt(nodes)
    want = np.sin(np.pi * r) / r if odd else np.cos(np.pi * r)
    fit = np.polynomial.chebyshev.Chebyshev.fit(nodes, want, terms - 1, domain=[0, 0.25])
    return [float(v) for v in fit.convert(kind=np.polynomial.Polynomial).coef]


SIN_FIT = half_turn_fit(True, 6)
COS_FIT = half_turn_fit(False, 6)


def horner(x, coef):
    total = coef[-1] * x + coef[-2]
    for value in coef[-3::-1]:
        total = total * x + value
    return total


def far_first(i, n):
    half = n // 2
    return half + ((i + 1) // 2) * (1 - 2 * (i % 2))


def kernel(raw_hbm, slot_hbm, offs_hbm, slow_hbm, twid_hbm, table_hbm, out,
           raw, slot, offs, slow, twid, table, send_a, recv_a, spec, send_c, recv_c, wide,
           send_b, recv_b, columns, spectra, weights, curve, send_d, recv_d,
           ssem_a, rsem_a, ssem_b, rsem_b, ssem_c, rsem_c, ssem_d, rsem_d, load_sems):
    me_k = lax.axis_index("freq")
    me_o = lax.axis_index("offset")
    me_x, me_z = me_o // NZ, me_o % NZ

    def peer_k(i):
        return (me_k + far_first(i, NK)) % NK

    def peer_o(i):
        dz = far_first(i // NX, NZ)
        dx = far_first(i % NX, NX)
        return ((me_x + dx) % NX) * NZ + (me_z + dz) % NZ

    loads = [
        pltpu.make_async_copy(src, dst, load_sems.at[i])
        for i, (src, dst) in enumerate([
            (slot_hbm, slot), (raw_hbm, raw), (offs_hbm, offs), (slow_hbm, slow),
            (twid_hbm, twid), (table_hbm, table)])
    ]
    for load in loads:
        load.start()
    barrier = pltpu.get_barrier_semaphore()

    def greet_k(i, c):
        pl.semaphore_signal(barrier, inc=1, device_id=(peer_k(i), me_o), device_id_type=MESH)
        return c

    def greet_o(i, c):
        pl.semaphore_signal(barrier, inc=1, device_id=(me_k, peer_o(i)), device_id_type=MESH)
        return c

    lax.fori_loop(0, NO - 1, greet_o, 0)
    lax.fori_loop(0, NK - 1, greet_k, 0)

    def copy_k(src, dst, ssem, rsem, there, here):
        return pltpu.make_async_remote_copy(
            src_ref=src.at[there], dst_ref=dst.at[here], send_sem=ssem.at[there],
            recv_sem=rsem.at[here], device_id=(there, me_o), device_id_type=MESH)

    def copy_o(src, dst, ssem, rsem, there, here):
        return pltpu.make_async_remote_copy(
            src_ref=src.at[there], dst_ref=dst.at[here], send_sem=ssem.at[there],
            recv_sem=rsem.at[here], device_id=(me_k, there), device_id_type=MESH)

    class Exchange:
        def __init__(self, over_freq, *refs):
            self.make, self.count, self.peer, self.me = (
                (copy_k, NK - 1, peer_k, me_k) if over_freq else (copy_o, NO - 1, peer_o, me_o))
            self.refs = refs

        def each(self, act):
            def step(i, c):
                act(self.peer(i))
                return c
            lax.fori_loop(0, self.count, step, 0)

        def start(self):
            self.each(lambda there: self.make(*self.refs, there, self.me).start())
            self.refs[1][self.me] = self.refs[0][self.me]

        def arrive(self):
            self.each(lambda there: self.make(*self.refs, there, there).wait_recv())

        def leave(self):
            self.each(lambda there: self.make(*self.refs, there, self.me).wait_send())

    def halves(over_freq, *refs):
        return [Exchange(over_freq, *(ref.at[h] for ref in refs)) for h in range(2)]

    ex_a = halves(True, send_a, recv_a, ssem_a, rsem_a)
    ex_b = halves(True, send_b, recv_b, ssem_b, rsem_b)
    ex_c = halves(False, send_c, recv_c, ssem_c, rsem_c)
    ex_d = Exchange(False, send_d, recv_d, ssem_d, rsem_d)

    loads[0].wait()
    loads[1].wait()
    row_ids = lax.broadcasted_iota(jnp.int32, (G, HB * G), 1)

    def pick(h):
        for part in range(2):
            chosen = jnp.concatenate([
                jnp.where(slot[:, 2 * kk + h:2 * kk + h + 1] == row_ids, 1.0, 0.0).astype(BF16)
                for kk in range(8 * part, 8 * part + 8)
            ], axis=0)
            rows = jnp.dot(chosen, raw[...], preferred_element_type=F32).astype(BF16)
            send_a[h, 8 * part:8 * part + 8] = rows.reshape(8, G, 128)

    pick(0)
    pl.semaphore_wait(barrier, NO - 1 + NK - 1)
    ex_a[0].start()
    pick(1)
    ex_a[1].start()

    loads[2].wait()
    loads[3].wait()
    for half in range(2):
        row = slow[:, 128 * half:128 * half + 128].astype(F32) * CURVATURE
        curve[128 * half:128 * half + 128, :] = jnp.transpose(jnp.broadcast_to(row, (128, 128)))
    first = 64 * me_k + 8 * me_z + me_x
    second = 64 * me_k + 8 * me_z + 7 - me_x
    rates = [(2 * f + 1).astype(F32) * (1.0 / (2 * NT)) for f in (first, second)]

    def weigh(block, c):
        rows = pl.ds(pl.multiple_of(block * 16, 16), 16)
        low = pl.ds(pl.multiple_of(block * 16 + NP, 16), 16)
        steep = curve[rows, :]
        for part in range(NH // 256):
            lanes = slice(256 * part, 256 * part + 256)
            spread = jnp.concatenate([steep, steep], axis=1) * offs[:, lanes].astype(F32)
            delay = jnp.sqrt(APEX_TIME * APEX_TIME + spread * spread) - APEX_TIME
            for f in range(2):
                turns = delay * rates[f]
                r = turns - jnp.round(turns)
                r2 = r * r
                s = horner(r2, SIN_FIT) * r
                q = horner(r2, COS_FIT)
                weights[f, rows, lanes] = (1.0 - 2.0 * (s * s)).astype(BF16)
                weights[f, low, lanes] = (2.0 * (s * q)).astype(BF16)
        return c

    lax.fori_loop(0, NP // 16, weigh, 0)
    loads[4].wait()
    loads[5].wait()

    lane = lax.broadcasted_iota(jnp.int32, (128, 128), 1) // 32

    def transform(h):
        x = [
            jnp.concatenate([recv_a[h, 2 * d], recv_a[h, 2 * d + 1]], axis=1).astype(F32)
            for d in range(8)
        ]
        less = [x[d] - x[8 - d] for d in range(1, 4)]
        more = [x[d] + x[8 - d] for d in range(1, 4)]
        for b in range(4):
            m = 2 * b + 1
            yr = x[0]
            yi = x[4] * (-math.sin(math.pi * m / 2))
            for d in range(1, 4):
                yr = yr + less[d - 1] * math.cos(math.pi * d * m / 8)
                yi = yi - more[d - 1] * math.sin(math.pi * d * m / 8)
            tc = twid[b:b + 1, :]
            ts = twid[4 + b:5 + b, :]
            for side, value in enumerate([yr * tc + yi * ts, yi * tc - yr * ts]):
                high = value.astype(BF16)
                rest = (value - high.astype(F32)).astype(BF16)
                lanes = slice(256 * side, 256 * side + 256)
                spec[G * b:G * b + G, lanes] = high
                spec[128 + G * b:128 + G * b + G, lanes] = rest
        parts = []
        for c in range(4):
            both = lax.dot_general(table[128 * c:128 * c + 128, :], spec[...],
                                   (((1,), (1,)), ((), ())), preferred_element_type=F32)
            parts.append(both[:, 0:128] + both[:, 128:256])
        for b in range(4):
            total = None
            for c in range(4):
                moved = parts[c] if c == b else pltpu.roll(parts[c], (c - b) * 32 % 128, 1)
                total = moved if c == 0 else jnp.where(lane == c, moved, total)
            send_c[h, 8 * b:8 * b + 8] = total.reshape(NZ, NK, 128).astype(BF16)

    def regroup(h):
        wide[...] = recv_c[h].astype(F32).reshape(NO * NK, 128)
        for kk in range(NK):
            send_b[h, kk] = wide[pl.ds(kk, NO, stride=NK), :].astype(BF16)

    for h in range(2):
        ex_a[h].arrive()
        transform(h)
        ex_c[h].start()
    for h in range(2):
        ex_c[h].arrive()
        regroup(h)
        ex_b[h].start()
    for h in range(2):
        ex_b[h].arrive()
        for kk in range(NK):
            base = 2 * NO * kk + NO * h
            columns[base:base + NO, :] = recv_b[h, kk].astype(F32)
    for o in range(NO):
        spectra[HB * o:HB * o + HB, :] = columns[pl.ds(o, HB, stride=NO), :].astype(BF16)

    lane2 = lax.broadcasted_iota(jnp.int32, (64, 128), 1)
    for block in range(NP // 64):
        rows = slice(64 * block, 64 * block + 64)
        low = slice(NP + 64 * block, NP + 64 * block + 64)
        data = spectra[...]
        cosine = [jnp.dot(weights[f, rows, :], data, preferred_element_type=F32) for f in range(2)]
        sines = [jnp.dot(weights[f, low, :], data, preferred_element_type=F32) for f in range(2)]
        ca = jnp.where(lane2 < 64, cosine[0], cosine[1])
        sa = jnp.where(lane2 < 64, sines[0], sines[1])
        swapped = jnp.where(lane2 % 64 < 32, -pltpu.roll(sa, 96, 1), pltpu.roll(sa, 32, 1))
        panel = (ca + swapped) * (1.0 / math.sqrt(NH))
        send_d[8 * block:8 * block + 8] = panel.reshape(8, 8, 128).astype(send_d.dtype)

    ex_d.start()
    ex_d.arrive()
    for o in range(NO):
        one = recv_d[o].astype(F32)
        f0 = 8 * (o % NZ) + o // NZ
        f1 = 8 * (o % NZ) + 7 - o // NZ
        out[pl.ds(f0, 8, stride=64), :] = one[:, 0:64]
        out[pl.ds(f1, 8, stride=64), :] = one[:, 64:128]

    for ex in ex_a + ex_b + ex_c + [ex_d]:
        ex.leave()


def local(raw_traces, trace_slot, offset_index, slowness_index):
    table, twiddle = dft_tables()
    dma = pltpu.SemaphoreType.DMA
    got = pl.pallas_call(
        kernel,
        out_shape=jax.ShapeDtypeStruct((8 * 64, 64), F32),
        in_specs=[pl.BlockSpec(memory_space=pltpu.HBM)] * 6,
        out_specs=pl.BlockSpec(memory_space=pltpu.VMEM),
        scratch_shapes=[
            pltpu.VMEM((HB * G, 128), BF16), pltpu.VMEM((G, HB), jnp.int32),
            pltpu.VMEM((1, NH), jnp.int32), pltpu.VMEM((1, NP), jnp.int32),
            pltpu.VMEM((8, 256), F32), pltpu.VMEM((512, 512), BF16),
            pltpu.VMEM((2, NK, G, 128), BF16), pltpu.VMEM((2, NK, G, 128), BF16),
            pltpu.VMEM((256, 512), BF16),
            pltpu.VMEM((2, NO, NK, 128), BF16), pltpu.VMEM((2, NO, NK, 128), BF16),
            pltpu.VMEM((NO * NK, 128), F32),
            pltpu.VMEM((2, NK, NO, 128), BF16), pltpu.VMEM((2, NK, NO, 128), BF16),
            pltpu.VMEM((NK * 2 * NO, 128), F32), pltpu.VMEM((NH, 128), BF16),
            pltpu.VMEM((2, 2 * NP, NH), BF16),
            pltpu.VMEM((NP, 128), F32),
            pltpu.VMEM((NO, 8, 128), BF16), pltpu.VMEM((NO, 8, 128), BF16),
            dma((2, NK)), dma((2, NK)), dma((2, NK)), dma((2, NK)),
            dma((2, NO)), dma((2, NO)), dma((NO,)), dma((NO,)), dma((6,)),
        ],
        compiler_params=pltpu.CompilerParams(collective_id=0, has_side_effects=True),
        name="radon",
    )(raw_traces, trace_slot, offset_index.reshape(1, NH), slowness_index.reshape(1, NP),
      jnp.asarray(twiddle), jnp.asarray(table, dtype=BF16))
    return got.reshape(8, 64, 64)


def solution(mesh):
    placed = (P("offset", "freq"), P(None, "offset"), P(), P())
    return jax.shard_map(
        local, mesh=mesh, in_specs=placed, out_specs=P("offset", "freq", None), check_vma=False
    )
```

```python
import functools
import math

import jax
import jax.numpy as jnp
import numpy as np
from jax import lax
from jax.experimental import pallas as pl
from jax.experimental.pallas import tpu as pltpu
from jax.sharding import PartitionSpec as P

NT = 2048
NF = 1024
NP = 256
G = 32
HB = 32
NH = 1024
NK = 16
NO = 32
NX = 4
NZ = 8
APEX_TIME = 100.0
CURVATURE = 0.0003
MESH = pl.DeviceIdType.MESH
F32 = jnp.float32
BF16 = jnp.bfloat16


def dft_tables():
    n = np.arange(256)[None, :]
    row = np.arange(128)
    a = (row % NK * NZ + row // NK)[:, None]
    t0 = 2 * np.pi * ((a * n) % 256) / 256
    t1 = 2 * np.pi * (((255 - a) * n) % 256) / 256
    rows = [
        np.concatenate([np.cos(t0), np.sin(t0)], 1),
        np.concatenate([-np.sin(t0), np.cos(t0)], 1),
        np.concatenate([np.cos(t1), np.sin(t1)], 1),
        np.concatenate([np.sin(t1), -np.cos(t1)], 1),
    ]
    table = np.concatenate(rows, 0)
    m = 2 * np.arange(4)[:, None] + 1
    turn = np.pi * (m * n) / 2048
    twiddle = np.concatenate([np.cos(turn), np.sin(turn)], 0) / math.sqrt(NT)
    return table.astype(np.float32), twiddle.astype(np.float32)


def half_turn_fit(odd, terms):
    nodes = 0.25 * (np.cos(np.pi * (np.arange(400) + 0.5) / 400) + 1) / 2
    r = np.sqrt(nodes)
    want = np.sin(np.pi * r) / r if odd else np.cos(np.pi * r)
    fit = np.polynomial.chebyshev.Chebyshev.fit(nodes, want, terms - 1, domain=[0, 0.25])
    return [float(v) for v in fit.convert(kind=np.polynomial.Polynomial).coef]


SIN_FIT = half_turn_fit(True, 6)
COS_FIT = half_turn_fit(False, 6)


def horner(x, coef):
    total = coef[-1] * x + coef[-2]
    for value in coef[-3::-1]:
        total = total * x + value
    return total


def far_first(n):
    return sorted(range(n), key=lambda d: -min(d, n - d))


def wrap(value, n):
    return jnp.where(value >= n, value - n, value)


def kernel(raw_hbm, slot_hbm, offs_hbm, slow_hbm, twid_hbm, table_hbm, out,
           raw, slot, offs, slow, twid, table, send_a, recv_a, spec, send_c, recv_c, wide,
           send_b, recv_b, columns, spectra, weights, curve, send_d, recv_d,
           ssem_a, rsem_a, ssem_b, rsem_b, ssem_c, rsem_c, ssem_d, rsem_d, load_sems):
    me_k = lax.axis_index("freq")
    me_o = lax.axis_index("offset")
    me_x, me_z = me_o // NZ, me_o % NZ

    peers_k = [wrap(me_k + d, NK) for d in far_first(NK) if d]
    peers_z = {d: wrap(me_z + d, NZ) for d in range(NZ)}
    peers_x = {d: wrap(me_x + d, NX) * NZ for d in range(NX)}
    peers_o = [
        peers_x[dx] + peers_z[dz]
        for dz in far_first(NZ) for dx in far_first(NX) if dx or dz
    ]

    loads = [
        pltpu.make_async_copy(src, dst, load_sems.at[i])
        for i, (src, dst) in enumerate([
            (slot_hbm, slot), (raw_hbm, raw), (offs_hbm, offs), (slow_hbm, slow),
            (twid_hbm, twid), (table_hbm, table)])
    ]
    for load in loads:
        load.start()
    barrier = pltpu.get_barrier_semaphore()

    for there in peers_o:
        pl.semaphore_signal(barrier, inc=1, device_id=(me_k, there), device_id_type=MESH)
    for there in peers_k:
        pl.semaphore_signal(barrier, inc=1, device_id=(there, me_o), device_id_type=MESH)

    class Exchange:
        def __init__(self, over_freq, src, dst, ssem, rsem):
            self.peers, self.me = (peers_k, me_k) if over_freq else (peers_o, me_o)
            self.over_freq, self.src, self.dst, self.ssem, self.rsem = over_freq, src, dst, ssem, rsem

        def start(self):
            for there in self.peers:
                pltpu.make_async_remote_copy(
                    src_ref=self.src.at[there], dst_ref=self.dst.at[self.me], send_sem=self.ssem,
                    recv_sem=self.rsem, device_id=(there, me_o) if self.over_freq else (me_k, there),
                    device_id_type=MESH).start()
            self.dst[self.me] = self.src[self.me]

        def arrive(self):
            part = self.dst.at[pl.ds(0, len(self.peers))]
            pltpu.make_async_copy(part, part, self.rsem).wait()

        def leave(self):
            part = self.src.at[pl.ds(0, len(self.peers))]
            pltpu.make_async_copy(part, part, self.ssem).wait()

    def halves(over_freq, *refs):
        return [Exchange(over_freq, *(ref.at[h] for ref in refs)) for h in range(2)]

    ex_a = halves(True, send_a, recv_a, ssem_a, rsem_a)
    ex_b = halves(True, send_b, recv_b, ssem_b, rsem_b)
    ex_c = halves(False, send_c, recv_c, ssem_c, rsem_c)
    ex_d = Exchange(False, send_d, recv_d, ssem_d, rsem_d)

    loads[0].wait()
    loads[1].wait()
    row_ids = lax.broadcasted_iota(jnp.int32, (G, HB * G), 1)

    def pick(h):
        for part in range(2):
            chosen = jnp.concatenate([
                jnp.where(slot[:, 2 * kk + h:2 * kk + h + 1] == row_ids, 1.0, 0.0).astype(BF16)
                for kk in range(8 * part, 8 * part + 8)
            ], axis=0)
            rows = jnp.dot(chosen, raw[...], preferred_element_type=F32).astype(BF16)
            send_a[h, 8 * part:8 * part + 8] = rows.reshape(8, G, 128)

    pick(0)
    pl.semaphore_wait(barrier, NO - 1 + NK - 1)
    ex_a[0].start()
    pick(1)
    ex_a[1].start()

    loads[2].wait()
    loads[3].wait()
    for half in range(2):
        row = slow[:, 128 * half:128 * half + 128].astype(F32) * CURVATURE
        curve[128 * half:128 * half + 128, :] = jnp.transpose(jnp.broadcast_to(row, (128, 128)))
    first = 64 * me_k + 8 * me_z + me_x
    second = 64 * me_k + 8 * me_z + 7 - me_x
    rates = [(2 * f + 1).astype(F32) * (1.0 / (2 * NT)) for f in (first, second)]

    def weigh(block, c):
        rows = pl.ds(pl.multiple_of(block * 16, 16), 16)
        low = pl.ds(pl.multiple_of(block * 16 + NP, 16), 16)
        steep = curve[rows, :]
        for part in range(NH // 256):
            lanes = slice(256 * part, 256 * part + 256)
            spread = jnp.concatenate([steep, steep], axis=1) * offs[:, lanes].astype(F32)
            delay = jnp.sqrt(APEX_TIME * APEX_TIME + spread * spread) - APEX_TIME
            for f in range(2):
                turns = delay * rates[f]
                r = turns - jnp.round(turns)
                r2 = r * r
                s = horner(r2, SIN_FIT) * r
                q = horner(r2, COS_FIT)
                weights[f, rows, lanes] = (1.0 - 2.0 * (s * s)).astype(BF16)
                weights[f, low, lanes] = (2.0 * (s * q)).astype(BF16)
        return c

    lax.fori_loop(0, NP // 16, weigh, 0)
    loads[4].wait()
    loads[5].wait()

    lane = lax.broadcasted_iota(jnp.int32, (128, 128), 1) // 32

    def transform(h):
        x = [
            jnp.concatenate([recv_a[h, 2 * d], recv_a[h, 2 * d + 1]], axis=1).astype(F32)
            for d in range(8)
        ]
        less = [x[d] - x[8 - d] for d in range(1, 4)]
        more = [x[d] + x[8 - d] for d in range(1, 4)]
        for b in range(4):
            m = 2 * b + 1
            yr = x[0]
            yi = x[4] * (-math.sin(math.pi * m / 2))
            for d in range(1, 4):
                yr = yr + less[d - 1] * math.cos(math.pi * d * m / 8)
                yi = yi - more[d - 1] * math.sin(math.pi * d * m / 8)
            tc = twid[b:b + 1, :]
            ts = twid[4 + b:5 + b, :]
            for side, value in enumerate([yr * tc + yi * ts, yi * tc - yr * ts]):
                high = value.astype(BF16)
                rest = (value - high.astype(F32)).astype(BF16)
                lanes = slice(256 * side, 256 * side + 256)
                spec[G * b:G * b + G, lanes] = high
                spec[128 + G * b:128 + G * b + G, lanes] = rest
        parts = []
        for c in range(4):
            both = lax.dot_general(table[128 * c:128 * c + 128, :], spec[...],
                                   (((1,), (1,)), ((), ())), preferred_element_type=F32)
            parts.append(both[:, 0:128] + both[:, 128:256])
        for b in range(4):
            total = None
            for c in range(4):
                moved = parts[c] if c == b else pltpu.roll(parts[c], (c - b) * 32 % 128, 1)
                total = moved if c == 0 else jnp.where(lane == c, moved, total)
            send_c[h, 8 * b:8 * b + 8] = total.reshape(NZ, NK, 128).astype(BF16)

    def regroup(h):
        wide[...] = recv_c[h].astype(F32).reshape(NO * NK, 128)
        for kk in range(NK):
            send_b[h, kk] = wide[pl.ds(kk, NO, stride=NK), :].astype(BF16)

    for h in range(2):
        ex_a[h].arrive()
        transform(h)
        ex_c[h].start()
    for h in range(2):
        ex_c[h].arrive()
        regroup(h)
        ex_b[h].start()
    for h in range(2):
        ex_b[h].arrive()
        for kk in range(NK):
            base = 2 * NO * kk + NO * h
            columns[base:base + NO, :] = recv_b[h, kk].astype(F32)
    for o in range(NO):
        spectra[HB * o:HB * o + HB, :] = columns[pl.ds(o, HB, stride=NO), :].astype(BF16)

    lane2 = lax.broadcasted_iota(jnp.int32, (64, 128), 1)
    for block in range(NP // 64):
        rows = slice(64 * block, 64 * block + 64)
        low = slice(NP + 64 * block, NP + 64 * block + 64)
        data = spectra[...]
        cosine = [jnp.dot(weights[f, rows, :], data, preferred_element_type=F32) for f in range(2)]
        sines = [jnp.dot(weights[f, low, :], data, preferred_element_type=F32) for f in range(2)]
        ca = jnp.where(lane2 < 64, cosine[0], cosine[1])
        sa = jnp.where(lane2 < 64, sines[0], sines[1])
        swapped = jnp.where(lane2 % 64 < 32, -pltpu.roll(sa, 96, 1), pltpu.roll(sa, 32, 1))
        panel = (ca + swapped) * (1.0 / math.sqrt(NH))
        send_d[8 * block:8 * block + 8] = panel.reshape(8, 8, 128).astype(send_d.dtype)

    ex_d.start()
    ex_d.arrive()
    for o in range(NO):
        one = recv_d[o].astype(F32)
        f0 = 8 * (o % NZ) + o // NZ
        f1 = 8 * (o % NZ) + 7 - o // NZ
        out[pl.ds(f0, 8, stride=64), :] = one[:, 0:64]
        out[pl.ds(f1, 8, stride=64), :] = one[:, 64:128]

    for ex in ex_a + ex_b + ex_c + [ex_d]:
        ex.leave()


def local(raw_traces, trace_slot, offset_index, slowness_index):
    table, twiddle = dft_tables()
    dma = pltpu.SemaphoreType.DMA
    got = pl.pallas_call(
        kernel,
        out_shape=jax.ShapeDtypeStruct((8 * 64, 64), F32),
        in_specs=[pl.BlockSpec(memory_space=pltpu.HBM)] * 6,
        out_specs=pl.BlockSpec(memory_space=pltpu.VMEM),
        scratch_shapes=[
            pltpu.VMEM((HB * G, 128), BF16), pltpu.VMEM((G, HB), jnp.int32),
            pltpu.VMEM((1, NH), jnp.int32), pltpu.VMEM((1, NP), jnp.int32),
            pltpu.VMEM((8, 256), F32), pltpu.VMEM((512, 512), BF16),
            pltpu.VMEM((2, NK, G, 128), BF16), pltpu.VMEM((2, NK, G, 128), BF16),
            pltpu.VMEM((256, 512), BF16),
            pltpu.VMEM((2, NO, NK, 128), BF16), pltpu.VMEM((2, NO, NK, 128), BF16),
            pltpu.VMEM((NO * NK, 128), F32),
            pltpu.VMEM((2, NK, NO, 128), BF16), pltpu.VMEM((2, NK, NO, 128), BF16),
            pltpu.VMEM((NK * 2 * NO, 128), F32), pltpu.VMEM((NH, 128), BF16),
            pltpu.VMEM((2, 2 * NP, NH), BF16),
            pltpu.VMEM((NP, 128), F32),
            pltpu.VMEM((NO, 8, 128), BF16), pltpu.VMEM((NO, 8, 128), BF16),
            dma((2,)), dma((2,)), dma((2,)), dma((2,)),
            dma((2,)), dma((2,)), dma(()), dma(()), dma((6,)),
        ],
        compiler_params=pltpu.CompilerParams(collective_id=0, has_side_effects=True),
        name="radon",
    )(raw_traces, trace_slot, offset_index.reshape(1, NH), slowness_index.reshape(1, NP),
      jnp.asarray(twiddle), jnp.asarray(table, dtype=BF16))
    return got.reshape(8, 64, 64)


def solution(mesh):
    placed = (P("offset", "freq"), P(None, "offset"), P(), P())
    return jax.shard_map(
        local, mesh=mesh, in_specs=placed, out_specs=P("offset", "freq", None), check_vma=False
    )
```

```python
import functools
import math

import jax
import jax.numpy as jnp
import numpy as np
from jax import lax
from jax.experimental import pallas as pl
from jax.experimental.pallas import tpu as pltpu
from jax.sharding import PartitionSpec as P

NT = 2048
NF = 1024
NP = 256
G = 32
HB = 32
NH = 1024
NK = 16
NO = 32
NX = 4
NZ = 8
APEX_TIME = 100.0
CURVATURE = 0.0003
MESH = pl.DeviceIdType.MESH
F32 = jnp.float32
BF16 = jnp.bfloat16


def dft_tables():
    n = np.arange(256)[None, :]
    row = np.arange(128)
    a = (row % NK * NZ + row // NK)[:, None]
    t0 = 2 * np.pi * ((a * n) % 256) / 256
    t1 = 2 * np.pi * (((255 - a) * n) % 256) / 256
    rows = [
        np.concatenate([np.cos(t0), np.sin(t0)], 1),
        np.concatenate([-np.sin(t0), np.cos(t0)], 1),
        np.concatenate([np.cos(t1), np.sin(t1)], 1),
        np.concatenate([np.sin(t1), -np.cos(t1)], 1),
    ]
    table = np.concatenate(rows, 0)
    m = 2 * np.arange(4)[:, None] + 1
    turn = np.pi * (m * n) / 2048
    twiddle = np.concatenate([np.cos(turn), np.sin(turn)], 0) / math.sqrt(NT)
    return table.astype(np.float32), twiddle.astype(np.float32)


def half_turn_fit(odd, terms):
    nodes = 0.25 * (np.cos(np.pi * (np.arange(400) + 0.5) / 400) + 1) / 2
    r = np.sqrt(nodes)
    want = np.sin(np.pi * r) / r if odd else np.cos(np.pi * r)
    fit = np.polynomial.chebyshev.Chebyshev.fit(nodes, want, terms - 1, domain=[0, 0.25])
    return [float(v) for v in fit.convert(kind=np.polynomial.Polynomial).coef]


SIN_FIT = half_turn_fit(True, 6)
COS_FIT = half_turn_fit(False, 6)


def horner(x, coef):
    total = coef[-1] * x + coef[-2]
    for value in coef[-3::-1]:
        total = total * x + value
    return total


def far_first(n):
    return sorted(range(n), key=lambda d: -min(d, n - d))


def wrap(value, n):
    return jnp.where(value >= n, value - n, value)


def kernel(raw_hbm, slot_hbm, offs_hbm, slow_hbm, twid_hbm, table_hbm, out,
           raw, slot, offs, slow, twid, table, send_a, recv_a, spec, send_c, recv_c, wide,
           send_b, recv_b, places, weights, curve, sums, send_d, recv_d,
           ssem_a, rsem_a, ssem_b, rsem_b, ssem_c, rsem_c, ssem_d, rsem_d, load_sems):
    me_k = lax.axis_index("freq")
    me_o = lax.axis_index("offset")
    me_x, me_z = me_o // NZ, me_o % NZ

    turns_k = far_first(NK)
    peers_k = [wrap(me_k + d, NK) for d in turns_k if d]
    peers_z = {d: wrap(me_z + d, NZ) for d in range(NZ)}
    peers_x = {d: wrap(me_x + d, NX) * NZ for d in range(NX)}
    peers_o = [
        peers_x[dx] + peers_z[dz]
        for dz in far_first(NZ) for dx in far_first(NX) if dx or dz
    ]

    loads = [
        pltpu.make_async_copy(src, dst, load_sems.at[i])
        for i, (src, dst) in enumerate([
            (slot_hbm, slot), (raw_hbm, raw), (offs_hbm, offs), (slow_hbm, slow),
            (twid_hbm, twid), (table_hbm, table)])
    ]
    for load in loads:
        load.start()
    barrier = pltpu.get_barrier_semaphore()

    for there in peers_o:
        pl.semaphore_signal(barrier, inc=1, device_id=(me_k, there), device_id_type=MESH)
    for there in peers_k:
        pl.semaphore_signal(barrier, inc=1, device_id=(there, me_o), device_id_type=MESH)

    class Exchange:
        def __init__(self, over_freq, src, dst, ssem, rsem):
            self.peers, self.me = (peers_k, me_k) if over_freq else (peers_o, me_o)
            self.over_freq, self.src, self.dst, self.ssem, self.rsem = over_freq, src, dst, ssem, rsem

        def send(self, there, slot):
            pltpu.make_async_remote_copy(
                src_ref=self.src.at[slot], dst_ref=self.dst.at[self.me], send_sem=self.ssem,
                recv_sem=self.rsem, device_id=(there, me_o) if self.over_freq else (me_k, there),
                device_id_type=MESH).start()

        def keep(self, slot):
            self.dst[self.me] = self.src[slot]

        def start(self):
            for there in self.peers:
                self.send(there, there)
            self.keep(self.me)

        def arrive(self):
            part = self.dst.at[pl.ds(0, len(self.peers))]
            pltpu.make_async_copy(part, part, self.rsem).wait()

        def leave(self):
            part = self.src.at[pl.ds(0, len(self.peers))]
            pltpu.make_async_copy(part, part, self.ssem).wait()

    def halves(over_freq, *refs):
        return [Exchange(over_freq, *(ref.at[h] for ref in refs)) for h in range(2)]

    ex_a = halves(True, send_a, recv_a, ssem_a, rsem_a)
    ex_b = halves(True, send_b, recv_b, ssem_b, rsem_b)
    ex_c = halves(False, send_c, recv_c, ssem_c, rsem_c)
    ex_d = Exchange(False, send_d, recv_d, ssem_d, rsem_d)

    loads[0].wait()
    loads[1].wait()
    row_ids = lax.broadcasted_iota(jnp.int32, (G, HB * G), 1)
    ahead = pltpu.roll(jnp.concatenate([slot[...]] * 4, axis=1), 4 * HB - 2 * me_k, 1)

    def pick(h, part):
        turns = turns_k[8 * part:8 * part + 8]
        chosen = jnp.concatenate([
            jnp.where(ahead[:, 2 * d + h:2 * d + h + 1] == row_ids, 1.0, 0.0).astype(BF16)
            for d in turns
        ], axis=0)
        rows = jnp.dot(chosen, raw[...], preferred_element_type=F32).astype(BF16)
        send_a[h, 8 * part:8 * part + 8] = rows.reshape(8, G, 128)

    def post(h, part):
        for i in range(8 * part, 8 * part + 8):
            if turns_k[i]:
                ex_a[h].send(peers_k[i], i)
            else:
                ex_a[h].keep(i)

    pick(0, 0)
    pl.semaphore_wait(barrier, NO - 1 + NK - 1)
    post(0, 0)
    for h, part in [(0, 1), (1, 0), (1, 1)]:
        pick(h, part)
        post(h, part)

    loads[2].wait()
    loads[3].wait()
    for half in range(2):
        row = slow[:, 128 * half:128 * half + 128].astype(F32) * CURVATURE
        curve[128 * half:128 * half + 128, :] = jnp.transpose(jnp.broadcast_to(row, (128, 128)))
    group = lax.broadcasted_iota(jnp.int32, (32, 128), 0)
    lane = lax.broadcasted_iota(jnp.int32, (32, 128), 1)
    eight = lax.broadcasted_iota(jnp.int32, (8, 128), 0)
    lane8 = lax.broadcasted_iota(jnp.int32, (8, 128), 1)
    grid = offs[...]
    place = None
    for size, digit in [(32.0, grid // 32), (1.0, grid % 32)]:
        digit = digit.astype(F32).astype(BF16)
        for m in range(4):
            wanted = 32 * m + 2 * (group % NK) + group // NK
            take = jnp.where(lane == wanted, 1.0, 0.0).astype(BF16)
            some = lax.dot_general(take, digit, (((1,), (1,)), ((), ())), preferred_element_type=F32)
            spread = jnp.where(lane8 % 32 == 4 * eight + m, size, 0.0).astype(BF16)
            term = jnp.dot(some.astype(BF16), spread, preferred_element_type=F32)
            place = term if place is None else place + term
    for tile in range(NH // 128):
        row = place[4 * tile:4 * tile + 1, :]
        for i in range(1, 4):
            row = jnp.where(lane[0:1] // 32 == i, place[4 * tile + i:4 * tile + i + 1, :], row)
        places[:, 128 * tile:128 * tile + 128] = row
    first = 64 * me_k + 8 * me_z + me_x
    second = 64 * me_k + 8 * me_z + 7 - me_x
    rates = [(2 * f + 1).astype(F32) * (1.0 / (2 * NT)) for f in (first, second)]

    def weigh(block, c):
        rows = pl.ds(pl.multiple_of(block * 16, 16), 16)
        low = pl.ds(pl.multiple_of(block * 16 + NP, 16), 16)
        steep = curve[rows, :]
        for part in range(NH // 256):
            lanes = slice(256 * part, 256 * part + 256)
            spread = jnp.concatenate([steep, steep], axis=1) * places[:, lanes]
            delay = jnp.sqrt(APEX_TIME * APEX_TIME + spread * spread) - APEX_TIME
            for f in range(2):
                turns = delay * rates[f]
                r = turns - jnp.round(turns)
                r2 = r * r
                s = horner(r2, SIN_FIT) * r
                q = horner(r2, COS_FIT)
                weights[f, rows, lanes] = (1.0 - 2.0 * (s * s)).astype(BF16)
                weights[f, low, lanes] = (2.0 * (s * q)).astype(BF16)
        return c

    lax.fori_loop(0, NP // 16, weigh, 0)
    loads[4].wait()
    loads[5].wait()

    lane = lax.broadcasted_iota(jnp.int32, (128, 128), 1) // 32

    def transform(h):
        x = [
            jnp.concatenate([recv_a[h, 2 * d], recv_a[h, 2 * d + 1]], axis=1).astype(F32)
            for d in range(8)
        ]
        less = [x[d] - x[8 - d] for d in range(1, 4)]
        more = [x[d] + x[8 - d] for d in range(1, 4)]
        for b in range(4):
            m = 2 * b + 1
            yr = x[0]
            yi = x[4] * (-math.sin(math.pi * m / 2))
            for d in range(1, 4):
                yr = yr + less[d - 1] * math.cos(math.pi * d * m / 8)
                yi = yi - more[d - 1] * math.sin(math.pi * d * m / 8)
            tc = twid[b:b + 1, :]
            ts = twid[4 + b:5 + b, :]
            for side, value in enumerate([yr * tc + yi * ts, yi * tc - yr * ts]):
                high = value.astype(BF16)
                rest = (value - high.astype(F32)).astype(BF16)
                lanes = slice(256 * side, 256 * side + 256)
                spec[G * b:G * b + G, lanes] = high
                spec[128 + G * b:128 + G * b + G, lanes] = rest
        parts = []
        for c in range(4):
            both = lax.dot_general(table[128 * c:128 * c + 128, :], spec[...],
                                   (((1,), (1,)), ((), ())), preferred_element_type=F32)
            parts.append(both[:, 0:128] + both[:, 128:256])
        for b in range(4):
            total = None
            for c in range(4):
                moved = parts[c] if c == b else pltpu.roll(parts[c], (c - b) * 32 % 128, 1)
                total = moved if c == 0 else jnp.where(lane == c, moved, total)
            send_c[h, 8 * b:8 * b + 8] = total.reshape(NZ, NK, 128).astype(BF16)

    def regroup(h):
        wide[...] = recv_c[h].astype(F32).reshape(NO * NK, 128)
        for kk in range(NK):
            send_b[h, kk] = wide[pl.ds(kk, NO, stride=NK), :].astype(BF16)

    for h in range(2):
        ex_a[h].arrive()
        transform(h)
        ex_c[h].start()
    for h in range(2):
        ex_c[h].arrive()
        regroup(h)
        ex_b[h].start()

    def merged(rows, h, side):
        data = recv_b[h].reshape(NH // 2, 128)
        lanes = slice(NH // 2 * h, NH // 2 * h + NH // 2)
        both = [jnp.dot(weights[f, rows, lanes], data, preferred_element_type=F32) for f in range(2)]
        return jnp.where(side, both[0], both[1])

    side = lax.broadcasted_iota(jnp.int32, (64, 128), 1)
    ex_b[0].arrive()
    for block in range(2 * NP // 64):
        rows = slice(64 * block, 64 * block + 64)
        sums[rows, :] = merged(rows, 0, side < 64)
    ex_b[1].arrive()
    for dx in far_first(NX):
        start = peers_x[dx] * 8
        rows = pl.ds(pl.multiple_of(start, 64), 64)
        low = pl.ds(pl.multiple_of(start + NP, 64), 64)
        ca = sums[rows, :] + merged(rows, 1, side < 64)
        sa = sums[low, :] + merged(low, 1, side < 64)
        swapped = jnp.where(side % 64 < 32, -pltpu.roll(sa, 96, 1), pltpu.roll(sa, 32, 1))
        panel = (ca + swapped) * (1.0 / math.sqrt(NH))
        send_d[pl.ds(peers_x[dx], 8)] = panel.reshape(8, 8, 128).astype(BF16)
        for dz in far_first(NZ):
            there = peers_x[dx] + peers_z[dz]
            if dx or dz:
                ex_d.send(there, there)
            else:
                ex_d.keep(there)
    ex_d.arrive()
    for o in range(NO):
        one = recv_d[o].astype(F32)
        f0 = 8 * (o % NZ) + o // NZ
        f1 = 8 * (o % NZ) + 7 - o // NZ
        out[pl.ds(f0, 8, stride=64), :] = one[:, 0:64]
        out[pl.ds(f1, 8, stride=64), :] = one[:, 64:128]

    for ex in ex_a + ex_b + ex_c + [ex_d]:
        ex.leave()


def local(raw_traces, trace_slot, offset_index, slowness_index):
    table, twiddle = dft_tables()
    dma = pltpu.SemaphoreType.DMA
    got = pl.pallas_call(
        kernel,
        out_shape=jax.ShapeDtypeStruct((8 * 64, 64), F32),
        in_specs=[pl.BlockSpec(memory_space=pltpu.HBM)] * 6,
        out_specs=pl.BlockSpec(memory_space=pltpu.VMEM),
        scratch_shapes=[
            pltpu.VMEM((HB * G, 128), BF16), pltpu.VMEM((G, HB), jnp.int32),
            pltpu.VMEM((8, 128), jnp.int32), pltpu.VMEM((1, NP), jnp.int32),
            pltpu.VMEM((8, 256), F32), pltpu.VMEM((512, 512), BF16),
            pltpu.VMEM((2, NK, G, 128), BF16), pltpu.VMEM((2, NK, G, 128), BF16),
            pltpu.VMEM((256, 512), BF16),
            pltpu.VMEM((2, NO, NK, 128), BF16), pltpu.VMEM((2, NO, NK, 128), BF16),
            pltpu.VMEM((NO * NK, 128), F32),
            pltpu.VMEM((2, NK, NO, 128), BF16), pltpu.VMEM((2, NK, NO, 128), BF16),
            pltpu.VMEM((1, NH), F32),
            pltpu.VMEM((2, 2 * NP, NH), BF16),
            pltpu.VMEM((NP, 128), F32), pltpu.VMEM((2 * NP, 128), F32),
            pltpu.VMEM((NO, 8, 128), BF16), pltpu.VMEM((NO, 8, 128), BF16),
            dma((2,)), dma((2,)), dma((2,)), dma((2,)),
            dma((2,)), dma((2,)), dma(()), dma(()), dma((6,)),
        ],
        compiler_params=pltpu.CompilerParams(collective_id=0, has_side_effects=True),
        name="radon",
    )(raw_traces, trace_slot, offset_index.reshape(8, 128), slowness_index.reshape(1, NP),
      jnp.asarray(twiddle), jnp.asarray(table, dtype=BF16))
    return got.reshape(8, 64, 64)


def solution(mesh):
    placed = (P("offset", "freq"), P(None, "offset"), P(), P())
    return jax.shard_map(
        local, mesh=mesh, in_specs=placed, out_specs=P("offset", "freq", None), check_vma=False
    )
```

```python
import functools
import math

import jax
import jax.numpy as jnp
import numpy as np
from jax import lax
from jax.experimental import pallas as pl
from jax.experimental.pallas import tpu as pltpu
from jax.sharding import PartitionSpec as P

NT = 2048
NF = 1024
NP = 256
G = 32
HB = 32
NH = 1024
NK = 16
NO = 32
NX = 4
NZ = 8
APEX_TIME = 100.0
CURVATURE = 0.0003
MESH = pl.DeviceIdType.MESH
F32 = jnp.float32
BF16 = jnp.bfloat16


def dft_tables():
    n = np.arange(256)[None, :]
    row = np.arange(128)
    a = (row % NK * NZ + row // NK)[:, None]
    t0 = 2 * np.pi * ((a * n) % 256) / 256
    t1 = 2 * np.pi * (((255 - a) * n) % 256) / 256
    rows = [
        np.concatenate([np.cos(t0), np.sin(t0)], 1),
        np.concatenate([-np.sin(t0), np.cos(t0)], 1),
        np.concatenate([np.cos(t1), np.sin(t1)], 1),
        np.concatenate([np.sin(t1), -np.cos(t1)], 1),
    ]
    table = np.concatenate(rows, 0)
    m = 2 * np.arange(4)[:, None] + 1
    turn = np.pi * (m * n) / 2048
    twiddle = np.concatenate([np.cos(turn), np.sin(turn)], 0) / math.sqrt(NT)
    return table.astype(np.float32), twiddle.astype(np.float32)


def half_turn_fit(odd, terms):
    nodes = 0.25 * (np.cos(np.pi * (np.arange(400) + 0.5) / 400) + 1) / 2
    r = np.sqrt(nodes)
    want = np.sin(np.pi * r) / r if odd else np.cos(np.pi * r)
    fit = np.polynomial.chebyshev.Chebyshev.fit(nodes, want, terms - 1, domain=[0, 0.25])
    return [float(v) for v in fit.convert(kind=np.polynomial.Polynomial).coef]


SIN_FIT = half_turn_fit(True, 6)
COS_FIT = half_turn_fit(False, 6)


def horner(x, coef):
    total = coef[-1] * x + coef[-2]
    for value in coef[-3::-1]:
        total = total * x + value
    return total


def far_first(n):
    return sorted(range(n), key=lambda d: -min(d, n - d))


def wrap(value, n):
    return jnp.where(value >= n, value - n, value)


def kernel(raw_hbm, slot_hbm, offs_hbm, slow_hbm, twid_hbm, table_hbm, out,
           raw, slot, offs, slow, twid, table, send_a, recv_a, spec, send_c, recv_c, wide,
           send_b, recv_b, places, weights, curve, sums, send_d, recv_d,
           ssem_a, rsem_a, ssem_b, rsem_b, ssem_c, rsem_c, ssem_d, rsem_d, load_sems):
    me_k = lax.axis_index("freq")
    me_o = lax.axis_index("offset")
    me_x, me_z = me_o // NZ, me_o % NZ

    turns_k = far_first(NK)
    peers_k = [wrap(me_k + d, NK) for d in turns_k if d]
    peers_z = {d: wrap(me_z + d, NZ) for d in range(NZ)}
    peers_x = {d: wrap(me_x + d, NX) * NZ for d in range(NX)}
    peers_o = [
        peers_x[dx] + peers_z[dz]
        for dz in far_first(NZ) for dx in far_first(NX) if dx or dz
    ]

    loads = [
        pltpu.make_async_copy(src, dst, load_sems.at[i])
        for i, (src, dst) in enumerate([
            (slot_hbm, slot), (raw_hbm, raw), (offs_hbm, offs), (slow_hbm, slow),
            (twid_hbm, twid), (table_hbm, table)])
    ]
    for load in loads:
        load.start()
    barrier = pltpu.get_barrier_semaphore()

    for there in peers_o:
        pl.semaphore_signal(barrier, inc=1, device_id=(me_k, there), device_id_type=MESH)
    for there in peers_k:
        pl.semaphore_signal(barrier, inc=1, device_id=(there, me_o), device_id_type=MESH)

    class Exchange:
        def __init__(self, over_freq, src, dst, ssem, rsem):
            self.peers, self.me = (peers_k, me_k) if over_freq else (peers_o, me_o)
            self.over_freq, self.src, self.dst, self.ssem, self.rsem = over_freq, src, dst, ssem, rsem

        def send(self, there, slot):
            pltpu.make_async_remote_copy(
                src_ref=self.src.at[slot], dst_ref=self.dst.at[self.me], send_sem=self.ssem,
                recv_sem=self.rsem, device_id=(there, me_o) if self.over_freq else (me_k, there),
                device_id_type=MESH).start()

        def keep(self, slot):
            self.dst[self.me] = self.src[slot]

        def start(self):
            for there in self.peers:
                self.send(there, there)
            self.keep(self.me)

        def arrive(self):
            part = self.dst.at[pl.ds(0, len(self.peers))]
            pltpu.make_async_copy(part, part, self.rsem).wait()

        def leave(self):
            part = self.src.at[pl.ds(0, len(self.peers))]
            pltpu.make_async_copy(part, part, self.ssem).wait()

    def halves(over_freq, *refs):
        return [Exchange(over_freq, *(ref.at[h] for ref in refs)) for h in range(2)]

    ex_a = halves(True, send_a, recv_a, ssem_a, rsem_a)
    ex_b = halves(True, send_b, recv_b, ssem_b, rsem_b)
    ex_c = halves(False, send_c, recv_c, ssem_c, rsem_c)
    ex_d = Exchange(False, send_d, recv_d, ssem_d, rsem_d)

    loads[0].wait()
    row_ids = lax.broadcasted_iota(jnp.int32, (G, HB * G), 1)
    ahead = pltpu.roll(jnp.concatenate([slot[...]] * 4, axis=1), 4 * HB - 2 * me_k, 1)

    def choose(h, part):
        turns = turns_k[8 * part:8 * part + 8]
        return jnp.concatenate([
            jnp.where(ahead[:, 2 * d + h:2 * d + h + 1] == row_ids, 1.0, 0.0).astype(BF16)
            for d in turns
        ], axis=0)

    def pick(h, part, chosen):
        rows = jnp.dot(chosen, raw[...], preferred_element_type=F32).astype(BF16)
        send_a[h, 8 * part:8 * part + 8] = rows.reshape(8, G, 128)

    def post(h, part):
        for i in range(8 * part, 8 * part + 8):
            if turns_k[i]:
                ex_a[h].send(peers_k[i], i)
            else:
                ex_a[h].keep(i)

    chosen = choose(0, 0)
    loads[1].wait()
    pick(0, 0, chosen)
    pl.semaphore_wait(barrier, NO - 1 + NK - 1)
    post(0, 0)
    for h, part in [(0, 1), (1, 0), (1, 1)]:
        pick(h, part, choose(h, part))
        post(h, part)

    loads[2].wait()
    loads[3].wait()
    for half in range(2):
        row = slow[:, 128 * half:128 * half + 128].astype(F32) * CURVATURE
        curve[128 * half:128 * half + 128, :] = jnp.transpose(jnp.broadcast_to(row, (128, 128)))
    group = lax.broadcasted_iota(jnp.int32, (32, 128), 0)
    lane = lax.broadcasted_iota(jnp.int32, (32, 128), 1)
    eight = lax.broadcasted_iota(jnp.int32, (8, 128), 0)
    lane8 = lax.broadcasted_iota(jnp.int32, (8, 128), 1)
    grid = offs[...]
    place = None
    for size, digit in [(32.0, grid // 32), (1.0, grid % 32)]:
        digit = digit.astype(F32).astype(BF16)
        for m in range(4):
            wanted = 32 * m + 2 * (group % NK) + group // NK
            take = jnp.where(lane == wanted, 1.0, 0.0).astype(BF16)
            some = lax.dot_general(take, digit, (((1,), (1,)), ((), ())), preferred_element_type=F32)
            spread = jnp.where(lane8 % 32 == 4 * eight + m, size, 0.0).astype(BF16)
            term = jnp.dot(some.astype(BF16), spread, preferred_element_type=F32)
            place = term if place is None else place + term
    for tile in range(NH // 128):
        row = place[4 * tile:4 * tile + 1, :]
        for i in range(1, 4):
            row = jnp.where(lane[0:1] // 32 == i, place[4 * tile + i:4 * tile + i + 1, :], row)
        places[:, 128 * tile:128 * tile + 128] = row
    first = 64 * me_k + 8 * me_z + me_x
    second = 64 * me_k + 8 * me_z + 7 - me_x
    rates = [(2 * f + 1).astype(F32) * (1.0 / (2 * NT)) for f in (first, second)]

    def weigh(block, c):
        rows = pl.ds(pl.multiple_of(block * 16, 16), 16)
        low = pl.ds(pl.multiple_of(block * 16 + NP, 16), 16)
        steep = curve[rows, :]
        for part in range(NH // 256):
            lanes = slice(256 * part, 256 * part + 256)
            spread = jnp.concatenate([steep, steep], axis=1) * places[:, lanes]
            delay = jnp.sqrt(APEX_TIME * APEX_TIME + spread * spread) - APEX_TIME
            for f in range(2):
                turns = delay * rates[f]
                r = turns - jnp.round(turns)
                r2 = r * r
                s = horner(r2, SIN_FIT) * r
                q = horner(r2, COS_FIT)
                weights[f, rows, lanes] = (1.0 - 2.0 * (s * s)).astype(BF16)
                weights[f, low, lanes] = (2.0 * (s * q)).astype(BF16)
        return c

    lax.fori_loop(0, NP // 16, weigh, 0)
    loads[4].wait()
    loads[5].wait()

    lane = lax.broadcasted_iota(jnp.int32, (128, 128), 1) // 32

    def transform(h):
        for part in range(2):
            x = [recv_a[h, 2 * d + part].astype(F32) for d in range(8)]
            less = [x[d] - x[8 - d] for d in range(1, 4)]
            more = [x[d] + x[8 - d] for d in range(1, 4)]
            for b in range(4):
                m = 2 * b + 1
                yr = x[0]
                yi = x[4] * (-math.sin(math.pi * m / 2))
                for d in range(1, 4):
                    yr = yr + less[d - 1] * math.cos(math.pi * d * m / 8)
                    yi = yi - more[d - 1] * math.sin(math.pi * d * m / 8)
                tc = twid[b:b + 1, 128 * part:128 * part + 128]
                ts = twid[4 + b:5 + b, 128 * part:128 * part + 128]
                for half, value in enumerate([yr * tc + yi * ts, yi * tc - yr * ts]):
                    high = value.astype(BF16)
                    rest = (value - high.astype(F32)).astype(BF16)
                    lanes = slice(256 * half + 128 * part, 256 * half + 128 * part + 128)
                    spec[G * b:G * b + G, lanes] = high
                    spec[128 + G * b:128 + G * b + G, lanes] = rest
        whole = lax.dot_general(table[...], spec[...], (((1,), (1,)), ((), ())),
                                preferred_element_type=F32)
        whole = whole[:, 0:128] + whole[:, 128:256]
        parts = [whole[128 * c:128 * c + 128, :] for c in range(4)]
        for b in range(4):
            total = None
            for c in range(4):
                moved = parts[c] if c == b else pltpu.roll(parts[c], (c - b) * 32 % 128, 1)
                total = moved if c == 0 else jnp.where(lane == c, moved, total)
            send_c[h, 8 * b:8 * b + 8] = total.reshape(NZ, NK, 128).astype(BF16)

    def regroup(h):
        wide[...] = recv_c[h].astype(F32).reshape(NO * NK, 128)
        for kk in range(NK):
            send_b[h, kk] = wide[pl.ds(kk, NO, stride=NK), :].astype(BF16)

    for h in range(2):
        ex_a[h].arrive()
        transform(h)
        ex_c[h].start()
    for h in range(2):
        ex_c[h].arrive()
        regroup(h)
        ex_b[h].start()

    def merged(rows, h, side):
        data = recv_b[h].reshape(NH // 2, 128)
        lanes = slice(NH // 2 * h, NH // 2 * h + NH // 2)
        both = [jnp.dot(weights[f, rows, lanes], data, preferred_element_type=F32) for f in range(2)]
        return jnp.where(side, both[0], both[1])

    side = lax.broadcasted_iota(jnp.int32, (64, 128), 1)
    ex_b[0].arrive()
    for block in range(2 * NP // 64):
        rows = slice(64 * block, 64 * block + 64)
        sums[rows, :] = merged(rows, 0, side < 64)
    ex_b[1].arrive()
    for dx in far_first(NX):
        start = peers_x[dx] * 8
        rows = pl.ds(pl.multiple_of(start, 64), 64)
        low = pl.ds(pl.multiple_of(start + NP, 64), 64)
        ca = sums[rows, :] + merged(rows, 1, side < 64)
        sa = sums[low, :] + merged(low, 1, side < 64)
        swapped = jnp.where(side % 64 < 32, -pltpu.roll(sa, 96, 1), pltpu.roll(sa, 32, 1))
        panel = (ca + swapped) * (1.0 / math.sqrt(NH))
        send_d[pl.ds(peers_x[dx], 8)] = panel.reshape(8, 8, 128).astype(BF16)
        for dz in far_first(NZ):
            there = peers_x[dx] + peers_z[dz]
            if dx or dz:
                ex_d.send(there, there)
            else:
                ex_d.keep(there)
    ex_d.arrive()
    for o in range(NO):
        one = recv_d[o].astype(F32)
        f0 = 8 * (o % NZ) + o // NZ
        f1 = 8 * (o % NZ) + 7 - o // NZ
        out[pl.ds(f0, 8, stride=64), :] = one[:, 0:64]
        out[pl.ds(f1, 8, stride=64), :] = one[:, 64:128]

    for ex in ex_a + ex_b + ex_c + [ex_d]:
        ex.leave()


def local(raw_traces, trace_slot, offset_index, slowness_index):
    table, twiddle = dft_tables()
    dma = pltpu.SemaphoreType.DMA
    got = pl.pallas_call(
        kernel,
        out_shape=pltpu.VMEM((8 * 64, 64), F32),
        in_specs=[pl.BlockSpec(memory_space=pltpu.HBM)] * 6,
        out_specs=pl.BlockSpec(memory_space=pltpu.VMEM),
        scratch_shapes=[
            pltpu.VMEM((HB * G, 128), BF16), pltpu.VMEM((G, HB), jnp.int32),
            pltpu.VMEM((8, 128), jnp.int32), pltpu.VMEM((1, NP), jnp.int32),
            pltpu.VMEM((8, 256), F32), pltpu.VMEM((512, 512), BF16),
            pltpu.VMEM((2, NK, G, 128), BF16), pltpu.VMEM((2, NK, G, 128), BF16),
            pltpu.VMEM((256, 512), BF16),
            pltpu.VMEM((2, NO, NK, 128), BF16), pltpu.VMEM((2, NO, NK, 128), BF16),
            pltpu.VMEM((NO * NK, 128), F32),
            pltpu.VMEM((2, NK, NO, 128), BF16), pltpu.VMEM((2, NK, NO, 128), BF16),
            pltpu.VMEM((1, NH), F32),
            pltpu.VMEM((2, 2 * NP, NH), BF16),
            pltpu.VMEM((NP, 128), F32), pltpu.VMEM((2 * NP, 128), F32),
            pltpu.VMEM((NO, 8, 128), BF16), pltpu.VMEM((NO, 8, 128), BF16),
            dma((2,)), dma((2,)), dma((2,)), dma((2,)),
            dma((2,)), dma((2,)), dma(()), dma(()), dma((6,)),
        ],
        compiler_params=pltpu.CompilerParams(collective_id=0, has_side_effects=True, vmem_limit_bytes=16 * 1024 * 1024),
        name="radon",
    )(*(pltpu.with_memory_space_constraint(v, pltpu.HBM) for v in (
        raw_traces, trace_slot, offset_index.reshape(8, 128), slowness_index.reshape(1, NP),
        jnp.asarray(twiddle), jnp.asarray(table, dtype=BF16))))
    return got.reshape(8, 64, 64)


def solution(mesh):
    placed = (P("offset", "freq"), P(None, "offset"), P(), P())
    return jax.shard_map(
        local, mesh=mesh, in_specs=placed, out_specs=P("offset", "freq", None), check_vma=False
    )
```

```python
import functools
import math

import jax
import jax.numpy as jnp
import numpy as np
from jax import lax
from jax.experimental import pallas as pl
from jax.experimental.pallas import tpu as pltpu
from jax.sharding import PartitionSpec as P

NT = 2048
NF = 1024
NP = 256
G = 32
HB = 32
NH = 1024
NK = 16
NO = 32
NX = 4
NZ = 8
APEX_TIME = 100.0
CURVATURE = 0.0003
MESH = pl.DeviceIdType.MESH
F32 = jnp.float32
BF16 = jnp.bfloat16


def dft_tables():
    n = np.arange(256)[None, :]
    row = np.arange(128)
    a = (row % NK * NZ + row // NK)[:, None]
    t0 = 2 * np.pi * ((a * n) % 256) / 256
    t1 = 2 * np.pi * (((255 - a) * n) % 256) / 256
    rows = [
        np.concatenate([np.cos(t0), np.sin(t0)], 1),
        np.concatenate([-np.sin(t0), np.cos(t0)], 1),
        np.concatenate([np.cos(t1), np.sin(t1)], 1),
        np.concatenate([np.sin(t1), -np.cos(t1)], 1),
    ]
    table = np.concatenate(rows, 0)
    m = 2 * np.arange(4)[:, None] + 1
    turn = np.pi * (m * n) / 2048
    twiddle = np.concatenate([np.cos(turn), np.sin(turn)], 0) / math.sqrt(NT)
    return table.astype(np.float32), twiddle.astype(np.float32)


def half_turn_fit(odd, terms):
    nodes = 0.25 * (np.cos(np.pi * (np.arange(400) + 0.5) / 400) + 1) / 2
    r = np.sqrt(nodes)
    want = np.sin(np.pi * r) / r if odd else np.cos(np.pi * r)
    fit = np.polynomial.chebyshev.Chebyshev.fit(nodes, want, terms - 1, domain=[0, 0.25])
    return [float(v) for v in fit.convert(kind=np.polynomial.Polynomial).coef]


SIN_FIT = half_turn_fit(True, 6)
COS_FIT = half_turn_fit(False, 6)


def horner(x, coef):
    total = coef[-1] * x + coef[-2]
    for value in coef[-3::-1]:
        total = total * x + value
    return total


def far_first(n):
    return sorted(range(n), key=lambda d: -min(d, n - d))


def wrap(value, n):
    return jnp.where(value >= n, value - n, value)


def kernel(raw_hbm, slot_hbm, offs_hbm, slow_hbm, twid_hbm, table_hbm, out,
           raw, slot, offs, slow, twid, table, send_a, recv_a, spec, send_c, recv_c, wide,
           send_b, recv_b, places, weights, curve, sums, send_d, recv_d,
           ssem_a, rsem_a, ssem_b, rsem_b, ssem_c, rsem_c, ssem_d, rsem_d, load_sems, plane_sem):
    me_k = lax.axis_index("freq")
    me_o = lax.axis_index("offset")
    me_x, me_z = me_o // NZ, me_o % NZ

    turns_k = far_first(NK)
    peers_k = [wrap(me_k + d, NK) for d in turns_k if d]
    peers_z = {d: wrap(me_z + d, NZ) for d in range(NZ)}
    peers_x = {d: wrap(me_x + d, NX) * NZ for d in range(NX)}
    peers_o = [
        peers_x[dx] + peers_z[dz]
        for dz in far_first(NZ) for dx in far_first(NX) if dx or dz
    ]

    loads = [
        pltpu.make_async_copy(src, dst, load_sems.at[i])
        for i, (src, dst) in enumerate([
            (slot_hbm, slot), (raw_hbm, raw), (offs_hbm, offs), (slow_hbm, slow),
            (twid_hbm, twid), (table_hbm, table)])
    ]
    barrier = pltpu.get_barrier_semaphore()
    loads[0].start()
    loads[1].start()

    for there in peers_k:
        pl.semaphore_signal(barrier, inc=1, device_id=(there, me_o), device_id_type=MESH)
    line_z = [me_x * NZ + peers_z[d] for d in far_first(NZ) if d]
    line_x = [peers_x[d] + me_z for d in far_first(NX) if d]
    for there in line_z + line_x:
        pl.semaphore_signal(barrier, inc=1, device_id=(me_k, there), device_id_type=MESH)
    for load in loads[2:]:
        load.start()

    class Exchange:
        def __init__(self, over_freq, src, dst, ssem, rsem):
            self.peers, self.me = (peers_k, me_k) if over_freq else (peers_o, me_o)
            self.over_freq, self.src, self.dst, self.ssem, self.rsem = over_freq, src, dst, ssem, rsem

        def send(self, there, slot):
            pltpu.make_async_remote_copy(
                src_ref=self.src.at[slot], dst_ref=self.dst.at[self.me], send_sem=self.ssem,
                recv_sem=self.rsem, device_id=(there, me_o) if self.over_freq else (me_k, there),
                device_id_type=MESH).start()

        def keep(self, slot):
            self.dst[self.me] = self.src[slot]

        def start(self):
            for there in self.peers:
                self.send(there, there)
            self.keep(self.me)

        def arrive(self):
            part = self.dst.at[pl.ds(0, len(self.peers))]
            pltpu.make_async_copy(part, part, self.rsem).wait()

        def leave(self):
            part = self.src.at[pl.ds(0, len(self.peers))]
            pltpu.make_async_copy(part, part, self.ssem).wait()

    def halves(over_freq, *refs):
        return [Exchange(over_freq, *(ref.at[h] for ref in refs)) for h in range(2)]

    ex_a = halves(True, send_a, recv_a, ssem_a, rsem_a)
    ex_b = halves(True, send_b, recv_b, ssem_b, rsem_b)
    ex_c = halves(False, send_c, recv_c, ssem_c, rsem_c)
    ex_d = Exchange(False, send_d, recv_d, ssem_d, rsem_d)

    loads[0].wait()
    row_ids = lax.broadcasted_iota(jnp.int32, (G, HB * G), 1)
    ahead = pltpu.roll(jnp.concatenate([slot[...]] * 4, axis=1), 4 * HB - 2 * me_k, 1)

    def choose(h, part):
        turns = turns_k[8 * part:8 * part + 8]
        return jnp.concatenate([
            jnp.where(ahead[:, 2 * d + h:2 * d + h + 1] == row_ids, 1.0, 0.0).astype(BF16)
            for d in turns
        ], axis=0)

    def pick(h, part, chosen):
        rows = jnp.dot(chosen, raw[...], preferred_element_type=F32).astype(BF16)
        send_a[h, 8 * part:8 * part + 8] = rows.reshape(8, G, 128)

    def post(h, part):
        for i in range(8 * part, 8 * part + 8):
            if turns_k[i]:
                ex_a[h].send(peers_k[i], i)
            else:
                ex_a[h].keep(i)

    chosen = choose(0, 0)
    loads[1].wait()
    pick(0, 0, chosen)
    pl.semaphore_wait(barrier, NK - 1 + NZ - 1 + NX - 1)
    post(0, 0)
    for there in line_x:
        pl.semaphore_signal(plane_sem, inc=1, device_id=(me_k, there), device_id_type=MESH)
    for h, part in [(0, 1), (1, 0), (1, 1)]:
        pick(h, part, choose(h, part))
        post(h, part)

    loads[2].wait()
    loads[3].wait()
    for half in range(2):
        row = slow[:, 128 * half:128 * half + 128].astype(F32) * CURVATURE
        curve[128 * half:128 * half + 128, :] = jnp.transpose(jnp.broadcast_to(row, (128, 128)))
    group = lax.broadcasted_iota(jnp.int32, (32, 128), 0)
    lane = lax.broadcasted_iota(jnp.int32, (32, 128), 1)
    eight = lax.broadcasted_iota(jnp.int32, (8, 128), 0)
    lane8 = lax.broadcasted_iota(jnp.int32, (8, 128), 1)
    grid = offs[...]
    place = None
    for size, digit in [(32.0, grid // 32), (1.0, grid % 32)]:
        digit = digit.astype(F32).astype(BF16)
        for m in range(4):
            wanted = 32 * m + 2 * (group % NK) + group // NK
            take = jnp.where(lane == wanted, 1.0, 0.0).astype(BF16)
            some = lax.dot_general(take, digit, (((1,), (1,)), ((), ())), preferred_element_type=F32)
            spread = jnp.where(lane8 % 32 == 4 * eight + m, size, 0.0).astype(BF16)
            term = jnp.dot(some.astype(BF16), spread, preferred_element_type=F32)
            place = term if place is None else place + term
    for tile in range(NH // 128):
        row = place[4 * tile:4 * tile + 1, :]
        for i in range(1, 4):
            row = jnp.where(lane[0:1] // 32 == i, place[4 * tile + i:4 * tile + i + 1, :], row)
        places[:, 128 * tile:128 * tile + 128] = row
    first = 64 * me_k + 8 * me_z + me_x
    second = 64 * me_k + 8 * me_z + 7 - me_x
    rates = [(2 * f + 1).astype(F32) * (1.0 / (2 * NT)) for f in (first, second)]

    def weigh(block, c):
        rows = pl.ds(pl.multiple_of(block * 16, 16), 16)
        low = pl.ds(pl.multiple_of(block * 16 + NP, 16), 16)
        steep = curve[rows, :]
        for part in range(NH // 256):
            lanes = slice(256 * part, 256 * part + 256)
            spread = jnp.concatenate([steep, steep], axis=1) * places[:, lanes]
            delay = jnp.sqrt(APEX_TIME * APEX_TIME + spread * spread) - APEX_TIME
            for f in range(2):
                turns = delay * rates[f]
                r = turns - jnp.round(turns)
                r2 = r * r
                s = horner(r2, SIN_FIT) * r
                q = horner(r2, COS_FIT)
                weights[f, rows, lanes] = (1.0 - 2.0 * (s * s)).astype(BF16)
                weights[f, low, lanes] = (2.0 * (s * q)).astype(BF16)
        return c

    lax.fori_loop(0, NP // 16, weigh, 0)
    loads[4].wait()
    loads[5].wait()

    lane = lax.broadcasted_iota(jnp.int32, (128, 128), 1) // 32

    def transform(h):
        for part in range(2):
            x = [recv_a[h, 2 * d + part].astype(F32) for d in range(8)]
            less = [x[d] - x[8 - d] for d in range(1, 4)]
            more = [x[d] + x[8 - d] for d in range(1, 4)]
            for b in range(4):
                m = 2 * b + 1
                yr = x[0]
                yi = x[4] * (-math.sin(math.pi * m / 2))
                for d in range(1, 4):
                    yr = yr + less[d - 1] * math.cos(math.pi * d * m / 8)
                    yi = yi - more[d - 1] * math.sin(math.pi * d * m / 8)
                tc = twid[b:b + 1, 128 * part:128 * part + 128]
                ts = twid[4 + b:5 + b, 128 * part:128 * part + 128]
                for half, value in enumerate([yr * tc + yi * ts, yi * tc - yr * ts]):
                    high = value.astype(BF16)
                    rest = (value - high.astype(F32)).astype(BF16)
                    lanes = slice(256 * half + 128 * part, 256 * half + 128 * part + 128)
                    spec[G * b:G * b + G, lanes] = high
                    spec[128 + G * b:128 + G * b + G, lanes] = rest
        whole = lax.dot_general(table[...], spec[...], (((1,), (1,)), ((), ())),
                                preferred_element_type=F32)
        whole = whole[:, 0:128] + whole[:, 128:256]
        parts = [whole[128 * c:128 * c + 128, :] for c in range(4)]
        for b in range(4):
            total = None
            for c in range(4):
                moved = parts[c] if c == b else pltpu.roll(parts[c], (c - b) * 32 % 128, 1)
                total = moved if c == 0 else jnp.where(lane == c, moved, total)
            send_c[h, 8 * b:8 * b + 8] = total.reshape(NZ, NK, 128).astype(BF16)

    def regroup(h):
        wide[...] = recv_c[h].astype(F32).reshape(NO * NK, 128)
        for kk in range(NK):
            send_b[h, kk] = wide[pl.ds(kk, NO, stride=NK), :].astype(BF16)

    for h in range(2):
        ex_a[h].arrive()
        transform(h)
        if h == 0:
            pl.semaphore_wait(plane_sem, NX - 1)
        ex_c[h].start()
    for h in range(2):
        ex_c[h].arrive()
        regroup(h)
        ex_b[h].start()

    def merged(rows, h, side):
        data = recv_b[h].reshape(NH // 2, 128)
        lanes = slice(NH // 2 * h, NH // 2 * h + NH // 2)
        both = [jnp.dot(weights[f, rows, lanes], data, preferred_element_type=F32) for f in range(2)]
        return jnp.where(side, both[0], both[1])

    side = lax.broadcasted_iota(jnp.int32, (64, 128), 1)
    ex_b[0].arrive()
    for block in range(2 * NP // 64):
        rows = slice(64 * block, 64 * block + 64)
        sums[rows, :] = merged(rows, 0, side < 64)
    ex_b[1].arrive()
    for dx in far_first(NX):
        start = peers_x[dx] * 8
        rows = pl.ds(pl.multiple_of(start, 64), 64)
        low = pl.ds(pl.multiple_of(start + NP, 64), 64)
        ca = sums[rows, :] + merged(rows, 1, side < 64)
        sa = sums[low, :] + merged(low, 1, side < 64)
        swapped = jnp.where(side % 64 < 32, -pltpu.roll(sa, 96, 1), pltpu.roll(sa, 32, 1))
        panel = (ca + swapped) * (1.0 / math.sqrt(NH))
        send_d[pl.ds(peers_x[dx], 8)] = panel.reshape(8, 8, 128).astype(BF16)
        for dz in far_first(NZ):
            there = peers_x[dx] + peers_z[dz]
            if dx or dz:
                ex_d.send(there, there)
            else:
                ex_d.keep(there)
    ex_d.arrive()
    for o in range(NO):
        one = recv_d[o].astype(F32)
        f0 = 8 * (o % NZ) + o // NZ
        f1 = 8 * (o % NZ) + 7 - o // NZ
        out[pl.ds(f0, 8, stride=64), :] = one[:, 0:64]
        out[pl.ds(f1, 8, stride=64), :] = one[:, 64:128]

    for ex in ex_a + ex_b + ex_c + [ex_d]:
        ex.leave()


def local(raw_traces, trace_slot, offset_index, slowness_index):
    table, twiddle = dft_tables()
    dma = pltpu.SemaphoreType.DMA
    got = pl.pallas_call(
        kernel,
        out_shape=pltpu.VMEM((8 * 64, 64), F32),
        in_specs=[pl.BlockSpec(memory_space=pltpu.HBM)] * 6,
        out_specs=pl.BlockSpec(memory_space=pltpu.VMEM),
        scratch_shapes=[
            pltpu.VMEM((HB * G, 128), BF16), pltpu.VMEM((G, HB), jnp.int32),
            pltpu.VMEM((8, 128), jnp.int32), pltpu.VMEM((1, NP), jnp.int32),
            pltpu.VMEM((8, 256), F32), pltpu.VMEM((512, 512), BF16),
            pltpu.VMEM((2, NK, G, 128), BF16), pltpu.VMEM((2, NK, G, 128), BF16),
            pltpu.VMEM((256, 512), BF16),
            pltpu.VMEM((2, NO, NK, 128), BF16), pltpu.VMEM((2, NO, NK, 128), BF16),
            pltpu.VMEM((NO * NK, 128), F32),
            pltpu.VMEM((2, NK, NO, 128), BF16), pltpu.VMEM((2, NK, NO, 128), BF16),
            pltpu.VMEM((1, NH), F32),
            pltpu.VMEM((2, 2 * NP, NH), BF16),
            pltpu.VMEM((NP, 128), F32), pltpu.VMEM((2 * NP, 128), F32),
            pltpu.VMEM((NO, 8, 128), BF16), pltpu.VMEM((NO, 8, 128), BF16),
            dma((2,)), dma((2,)), dma((2,)), dma((2,)),
            dma((2,)), dma((2,)), dma(()), dma(()), dma((6,)), pltpu.SemaphoreType.REGULAR,
        ],
        compiler_params=pltpu.CompilerParams(collective_id=0, has_side_effects=True, vmem_limit_bytes=16 * 1024 * 1024),
        name="radon",
    )(*(pltpu.with_memory_space_constraint(v, pltpu.HBM) for v in (
        raw_traces, trace_slot, offset_index.reshape(8, 128), slowness_index.reshape(1, NP),
        jnp.asarray(twiddle), jnp.asarray(table, dtype=BF16))))
    return got.reshape(8, 64, 64)


def solution(mesh):
    placed = (P("offset", "freq"), P(None, "offset"), P(), P())
    return jax.shard_map(
        local, mesh=mesh, in_specs=placed, out_specs=P("offset", "freq", None), check_vma=False
    )
```

```python
import functools
import math

import jax
import jax.numpy as jnp
import numpy as np
from jax import lax
from jax.experimental import pallas as pl
from jax.experimental.pallas import tpu as pltpu
from jax.sharding import PartitionSpec as P

NT = 2048
NF = 1024
NP = 256
G = 32
HB = 32
NH = 1024
NK = 16
NO = 32
NX = 4
NY = 8
NZ = 8
APEX_TIME = 100.0
CURVATURE = 0.0003
MESH = pl.DeviceIdType.MESH
F32 = jnp.float32
BF16 = jnp.bfloat16


def dft_tables():
    n = np.arange(256)[None, :]
    high = np.arange(64) // 8
    low = np.arange(64) % 8
    tables = []
    for core in range(2):
        same = 8 * (2 * low + core) + high
        other = 8 * (2 * high + 1 - core) + low
        a = np.concatenate([same, other])[:, None]
        t0 = 2 * np.pi * ((a * n) % 256) / 256
        t1 = 2 * np.pi * (((255 - a) * n) % 256) / 256
        rows = [
            np.concatenate([np.cos(t0), np.sin(t0)], 1),
            np.concatenate([-np.sin(t0), np.cos(t0)], 1),
            np.concatenate([np.cos(t1), np.sin(t1)], 1),
            np.concatenate([np.sin(t1), -np.cos(t1)], 1),
        ]
        tables.append(np.concatenate(rows, 0))
    m = 2 * np.arange(4)[:, None] + 1
    turn = np.pi * (m * n) / 2048
    twiddle = np.concatenate([np.cos(turn), np.sin(turn)], 0) / math.sqrt(NT)
    return np.stack(tables).astype(np.float32), twiddle.astype(np.float32)


def half_turn_fit(odd, terms):
    nodes = 0.25 * (np.cos(np.pi * (np.arange(400) + 0.5) / 400) + 1) / 2
    r = np.sqrt(nodes)
    want = np.sin(np.pi * r) / r if odd else np.cos(np.pi * r)
    fit = np.polynomial.chebyshev.Chebyshev.fit(nodes, want, terms - 1, domain=[0, 0.25])
    return [float(v) for v in fit.convert(kind=np.polynomial.Polynomial).coef]


SIN_FIT = half_turn_fit(True, 6)
COS_FIT = half_turn_fit(False, 6)


def horner(x, coef):
    total = coef[-1] * x + coef[-2]
    for value in coef[-3::-1]:
        total = total * x + value
    return total


def far_first(n):
    return sorted(range(n), key=lambda d: -min(d, n - d))


def wrap(value, n):
    return jnp.where(value >= n, value - n, value)


def kernel(raw_hbm, slot_hbm, offs_hbm, slow_hbm, twid_hbm, table_hbm, out,
           raw, slot, offs, slow, twid, table, send_a, recv_a, spec, wide,
           send_p, recv_p, send_r, recv_r, send_s, recv_s, send_t, recv_t, places, weights, curve, sums, send_d, recv_d,
           ssems, rsems, load_sems, plane_sem):
    me_k = lax.axis_index("freq")
    me_o = lax.axis_index("offset")
    me_x, me_z = me_o // NZ, me_o % NZ
    me_y = me_k // 2
    me_c = me_k - 2 * me_y

    turns_k = far_first(NK)
    peers_k = [wrap(me_k + d, NK) for d in turns_k if d]
    peers_z = {d: wrap(me_z + d, NZ) for d in range(NZ)}
    peers_x = {d: wrap(me_x + d, NX) * NZ for d in range(NX)}
    peers_o = [
        peers_x[dx] + peers_z[dz]
        for dz in far_first(NZ) for dx in far_first(NX) if dx or dz
    ]

    loads = [
        pltpu.make_async_copy(src, dst, load_sems.at[i])
        for i, (src, dst) in enumerate([
            (slot_hbm, slot), (raw_hbm, raw), (offs_hbm, offs), (slow_hbm, slow),
            (twid_hbm, twid), (table_hbm.at[me_c], table)])
    ]
    barrier = pltpu.get_barrier_semaphore()
    loads[0].start()
    loads[1].start()

    for there in peers_k:
        pl.semaphore_signal(barrier, inc=1, device_id=(there, me_o), device_id_type=MESH)
    line_z = [me_x * NZ + peers_z[d] for d in far_first(NZ) if d]
    line_x = [peers_x[d] + me_z for d in far_first(NX) if d]
    for there in line_z + line_x:
        pl.semaphore_signal(barrier, inc=1, device_id=(me_k, there), device_id_type=MESH)
    for load in loads[2:]:
        load.start()

    rings_y = [wrap(me_y + d, NY) for d in far_first(NY)]
    to_k = [((there, me_o), there) for there in peers_k]
    to_o = [((me_k, there), there) for there in peers_o]
    to_same = [((2 * there + me_c, me_o), there) for there in rings_y[:-1]]
    to_other = [((2 * there + 1 - me_c, me_o), there) for there in rings_y]
    exchanges = []

    class Exchange:
        def __init__(self, src, dst, peers, me):
            self.src, self.dst, self.peers, self.me = src, dst, peers, me
            self.ssem, self.rsem = ssems.at[len(exchanges)], rsems.at[len(exchanges)]
            exchanges.append(self)

        def send(self, device, slot):
            pltpu.make_async_remote_copy(
                src_ref=self.src.at[slot], dst_ref=self.dst.at[self.me], send_sem=self.ssem,
                recv_sem=self.rsem, device_id=device, device_id_type=MESH).start()

        def keep(self, slot):
            self.dst[self.me] = self.src[slot]

        def start(self):
            for device, slot in self.peers:
                self.send(device, slot)

        def arrive(self):
            part = self.dst.at[pl.ds(0, len(self.peers))]
            pltpu.make_async_copy(part, part, self.rsem).wait()

        def leave(self):
            part = self.src.at[pl.ds(0, len(self.peers))]
            pltpu.make_async_copy(part, part, self.ssem).wait()

    def halves(src, dst, peers, me):
        return [Exchange(src.at[h], dst.at[h], peers, me) for h in range(2)]

    ex_a = halves(send_a, recv_a, to_k, me_k)
    ex_p = halves(send_p, recv_p, to_o, me_o)
    ex_s = halves(send_s, recv_s, to_same, me_y)
    ex_r = halves(send_r, recv_r, to_other, me_y)
    ex_t = halves(send_t, recv_t, to_o, me_o)
    ex_d = Exchange(send_d, recv_d, to_o, me_o)

    loads[0].wait()
    row_ids = lax.broadcasted_iota(jnp.int32, (G, HB * G), 1)
    ahead = pltpu.roll(jnp.concatenate([slot[...]] * 4, axis=1), 4 * HB - 2 * me_k, 1)

    def choose(h, part):
        turns = turns_k[8 * part:8 * part + 8]
        return jnp.concatenate([
            jnp.where(ahead[:, 2 * d + h:2 * d + h + 1] == row_ids, 1.0, 0.0).astype(BF16)
            for d in turns
        ], axis=0)

    def pick(h, part, chosen):
        rows = jnp.dot(chosen, raw[...], preferred_element_type=F32).astype(BF16)
        send_a[h, 8 * part:8 * part + 8] = rows.reshape(8, G, 128)

    def post(h, part):
        for i in range(8 * part, 8 * part + 8):
            if turns_k[i]:
                ex_a[h].send((peers_k[i], me_o), i)
            else:
                ex_a[h].keep(i)

    chosen = choose(0, 0)
    loads[1].wait()
    pick(0, 0, chosen)
    pl.semaphore_wait(barrier, NK - 1 + NZ - 1 + NX - 1)
    post(0, 0)
    for there in line_x:
        pl.semaphore_signal(plane_sem, inc=1, device_id=(me_k, there), device_id_type=MESH)
    for h, part in [(0, 1), (1, 0), (1, 1)]:
        pick(h, part, choose(h, part))
        post(h, part)

    loads[2].wait()
    loads[3].wait()
    for half in range(2):
        row = slow[:, 128 * half:128 * half + 128].astype(F32) * CURVATURE
        curve[128 * half:128 * half + 128, :] = jnp.transpose(jnp.broadcast_to(row, (128, 128)))
    group = lax.broadcasted_iota(jnp.int32, (16, 128), 0)
    lane = lax.broadcasted_iota(jnp.int32, (16, 128), 1)
    eight = lax.broadcasted_iota(jnp.int32, (8, 128), 0)
    lane8 = lax.broadcasted_iota(jnp.int32, (8, 128), 1)
    deep = lax.broadcasted_iota(jnp.int32, (128, 128), 0)
    lane128 = lax.broadcasted_iota(jnp.int32, (128, 128), 1)
    grid = offs[...]
    digits = [(32.0, grid // 32), (1.0, grid % 32)]
    digits = [(size, digit.astype(F32).astype(BF16)) for size, digit in digits]
    place = None
    for size, digit in digits:
        for m in range(4):
            wanted = 32 * m + 2 * (2 * (group % NY) + me_c) + group // NY
            take = jnp.where(lane == wanted, 1.0, 0.0).astype(BF16)
            some = lax.dot_general(take, digit, (((1,), (1,)), ((), ())), preferred_element_type=F32)
            spread = jnp.where(lane8 % 32 == 4 * eight + m, size, 0.0).astype(BF16)
            term = jnp.dot(some.astype(BF16), spread, preferred_element_type=F32)
            place = term if place is None else place + term
    for h in range(2):
        wanted = (lane128 // 8 % 4) * 32 + 2 * (2 * (lane128 % 8) + 1 - me_c) + h
        other = None
        for size, digit in digits:
            take = jnp.where(deep == wanted, size, 0.0).astype(BF16)
            term = jnp.dot(digit, take, preferred_element_type=F32)
            other = term if other is None else other + term
        for source, base, start in [(place, NY * h, 512 * h), (other, 0, 512 * h + 256)]:
            for tile in range(2):
                at = base + 4 * tile
                row = source[at:at + 1, :]
                for i in range(1, 4):
                    row = jnp.where(lane[0:1] // 32 == i, source[at + i:at + i + 1, :], row)
                places[:, start + 128 * tile:start + 128 * tile + 128] = row
    first = 64 * me_k + 8 * me_z + me_x
    second = 64 * me_k + 8 * me_z + 7 - me_x
    rates = [(2 * f + 1).astype(F32) * (1.0 / (2 * NT)) for f in (first, second)]

    def weigh(block, c):
        rows = pl.ds(pl.multiple_of(block * 16, 16), 16)
        low = pl.ds(pl.multiple_of(block * 16 + NP, 16), 16)
        steep = curve[rows, :]
        for part in range(NH // 256):
            lanes = slice(256 * part, 256 * part + 256)
            spread = jnp.concatenate([steep, steep], axis=1) * places[:, lanes]
            delay = jnp.sqrt(APEX_TIME * APEX_TIME + spread * spread) - APEX_TIME
            for f in range(2):
                turns = delay * rates[f]
                r = turns - jnp.round(turns)
                r2 = r * r
                s = horner(r2, SIN_FIT) * r
                q = horner(r2, COS_FIT)
                weights[f, rows, lanes] = (1.0 - 2.0 * (s * s)).astype(BF16)
                weights[f, low, lanes] = (2.0 * (s * q)).astype(BF16)
        return c

    lax.fori_loop(0, NP // 16, weigh, 0)
    loads[4].wait()
    loads[5].wait()

    lane = lax.broadcasted_iota(jnp.int32, (128, 128), 1) // 32

    def transform(h):
        for part in range(2):
            x = [recv_a[h, 2 * d + part].astype(F32) for d in range(8)]
            less = [x[d] - x[8 - d] for d in range(1, 4)]
            more = [x[d] + x[8 - d] for d in range(1, 4)]
            for b in range(4):
                m = 2 * b + 1
                yr = x[0]
                yi = x[4] * (-math.sin(math.pi * m / 2))
                for d in range(1, 4):
                    yr = yr + less[d - 1] * math.cos(math.pi * d * m / 8)
                    yi = yi - more[d - 1] * math.sin(math.pi * d * m / 8)
                tc = twid[b:b + 1, 128 * part:128 * part + 128]
                ts = twid[4 + b:5 + b, 128 * part:128 * part + 128]
                for half, value in enumerate([yr * tc + yi * ts, yi * tc - yr * ts]):
                    high = value.astype(BF16)
                    rest = (value - high.astype(F32)).astype(BF16)
                    lanes = slice(256 * half + 128 * part, 256 * half + 128 * part + 128)
                    spec[G * b:G * b + G, lanes] = high
                    spec[128 + G * b:128 + G * b + G, lanes] = rest
        whole = lax.dot_general(table[...], spec[...], (((1,), (1,)), ((), ())),
                                preferred_element_type=F32)
        whole = whole[:, 0:128] + whole[:, 128:256]
        parts = [whole[128 * c:128 * c + 128, :] for c in range(4)]
        bottoms = []
        for b in range(4):
            total = None
            for c in range(4):
                moved = parts[c] if c == b else pltpu.roll(parts[c], (c - b) * 32 % 128, 1)
                total = moved if c == 0 else jnp.where(lane == c, moved, total)
            send_p[h, 8 * b:8 * b + 8] = total[0:64].reshape(NZ, NY, 128).astype(BF16)
            bottoms.append(total[64:128].reshape(NY, NZ, 128))
        for t in range(2):
            pair = jnp.concatenate(bottoms[2 * t:2 * t + 2], axis=1).astype(BF16)
            send_r[h, :, 16 * t:16 * t + 16, :] = pair

    def turn_p(h):
        wide[...] = recv_p[h].astype(F32).reshape(NO * NY, 128)
        for y in range(NY):
            send_s[h, y] = wide[pl.ds(y, NO, stride=NY), :].astype(BF16)

    def turn_r(h):
        wide[...] = recv_r[h].astype(F32).reshape(NO * NY, 128)
        for o in range(NO):
            send_t[h, o] = wide[pl.ds(o, NY, stride=NO), :].astype(BF16)

    for h in range(2):
        ex_a[h].arrive()
        transform(h)
        if h == 0:
            pl.semaphore_wait(plane_sem, NX - 1)
        ex_p[h].start()
        ex_r[h].start()
        ex_p[h].keep(me_o)
    for h in range(2):
        ex_r[h].arrive()
        turn_r(h)
        ex_t[h].start()
        ex_t[h].keep(me_o)
        ex_p[h].arrive()
        turn_p(h)
        ex_s[h].start()
        ex_s[h].keep(me_y)

    def merged(rows, h, side):
        data = jnp.concatenate(
            [recv_s[h].reshape(NH // 4, 128), recv_t[h].astype(F32).reshape(NH // 4, 128).astype(BF16)])
        lanes = slice(NH // 2 * h, NH // 2 * h + NH // 2)
        both = [jnp.dot(weights[f, rows, lanes], data, preferred_element_type=F32) for f in range(2)]
        return jnp.where(side, both[0], both[1])

    side = lax.broadcasted_iota(jnp.int32, (64, 128), 1)
    ex_s[0].arrive()
    ex_t[0].arrive()
    for block in range(2 * NP // 64):
        rows = slice(64 * block, 64 * block + 64)
        sums[rows, :] = merged(rows, 0, side < 64)
    ex_s[1].arrive()
    ex_t[1].arrive()
    for dx in far_first(NX):
        start = peers_x[dx] * 8
        rows = pl.ds(pl.multiple_of(start, 64), 64)
        low = pl.ds(pl.multiple_of(start + NP, 64), 64)
        ca = sums[rows, :] + merged(rows, 1, side < 64)
        sa = sums[low, :] + merged(low, 1, side < 64)
        swapped = jnp.where(side % 64 < 32, -pltpu.roll(sa, 96, 1), pltpu.roll(sa, 32, 1))
        panel = (ca + swapped) * (1.0 / math.sqrt(NH))
        send_d[pl.ds(peers_x[dx], 8)] = panel.reshape(8, 8, 128).astype(BF16)
        for dz in far_first(NZ):
            there = peers_x[dx] + peers_z[dz]
            if dx or dz:
                ex_d.send((me_k, there), there)
            else:
                ex_d.keep(there)
    ex_d.arrive()
    for o in range(NO):
        one = recv_d[o].astype(F32)
        f0 = 8 * (o % NZ) + o // NZ
        f1 = 8 * (o % NZ) + 7 - o // NZ
        out[pl.ds(f0, 8, stride=64), :] = one[:, 0:64]
        out[pl.ds(f1, 8, stride=64), :] = one[:, 64:128]

    for ex in exchanges:
        ex.leave()


def local(raw_traces, trace_slot, offset_index, slowness_index):
    table, twiddle = dft_tables()
    dma = pltpu.SemaphoreType.DMA
    got = pl.pallas_call(
        kernel,
        out_shape=pltpu.VMEM((8 * 64, 64), F32),
        in_specs=[pl.BlockSpec(memory_space=pltpu.HBM)] * 6,
        out_specs=pl.BlockSpec(memory_space=pltpu.VMEM),
        scratch_shapes=[
            pltpu.VMEM((HB * G, 128), BF16), pltpu.VMEM((G, HB), jnp.int32),
            pltpu.VMEM((8, 128), jnp.int32), pltpu.VMEM((1, NP), jnp.int32),
            pltpu.VMEM((8, 256), F32), pltpu.VMEM((512, 512), BF16),
            pltpu.VMEM((2, NK, G, 128), BF16), pltpu.VMEM((2, NK, G, 128), BF16),
            pltpu.VMEM((256, 512), BF16),
            pltpu.VMEM((NO * NY, 128), F32),
            pltpu.VMEM((2, NO, NY, 128), BF16), pltpu.VMEM((2, NO, NY, 128), BF16),
            pltpu.VMEM((2, NY, NO, 128), BF16), pltpu.VMEM((2, NY, NO, 128), BF16),
            pltpu.VMEM((2, NY, NO, 128), BF16), pltpu.VMEM((2, NY, NO, 128), BF16),
            pltpu.VMEM((2, NO, NY, 128), BF16), pltpu.VMEM((2, NO, NY, 128), BF16),
            pltpu.VMEM((1, NH), F32),
            pltpu.VMEM((2, 2 * NP, NH), BF16),
            pltpu.VMEM((NP, 128), F32), pltpu.VMEM((2 * NP, 128), F32),
            pltpu.VMEM((NO, 8, 128), BF16), pltpu.VMEM((NO, 8, 128), BF16),
            dma((11,)), dma((11,)), dma((6,)), pltpu.SemaphoreType.REGULAR,
        ],
        compiler_params=pltpu.CompilerParams(collective_id=0, has_side_effects=True, vmem_limit_bytes=16 * 1024 * 1024),
        name="radon",
    )(*(pltpu.with_memory_space_constraint(v, pltpu.HBM) for v in (
        raw_traces, trace_slot, offset_index.reshape(8, 128), slowness_index.reshape(1, NP),
        jnp.asarray(twiddle), jnp.asarray(table, dtype=BF16))))
    return got.reshape(8, 64, 64)


def solution(mesh):
    placed = (P("offset", "freq"), P(None, "offset"), P(), P())
    return jax.shard_map(
        local, mesh=mesh, in_specs=placed, out_specs=P("offset", "freq", None), check_vma=False
    )
```

```python
import functools
import math

import jax
import jax.numpy as jnp
import numpy as np
from jax import lax
from jax.experimental import pallas as pl
from jax.experimental.pallas import tpu as pltpu
from jax.sharding import PartitionSpec as P

NT = 2048
NF = 1024
NP = 256
G = 32
HB = 32
NH = 1024
NK = 16
NO = 32
NX = 4
NY = 8
NZ = 8
APEX_TIME = 100.0
CURVATURE = 0.0003
MESH = pl.DeviceIdType.MESH
F32 = jnp.float32
BF16 = jnp.bfloat16


def dft_tables():
    n = np.arange(256)[None, :]
    high = np.arange(64) // 8
    low = np.arange(64) % 8
    tables = []
    for core in range(2):
        same = 8 * (2 * low + core) + high
        other = 8 * (2 * high + 1 - core) + low
        a = np.concatenate([same, other])[:, None]
        t0 = 2 * np.pi * ((a * n) % 256) / 256
        t1 = 2 * np.pi * (((255 - a) * n) % 256) / 256
        rows = [
            np.concatenate([np.cos(t0), np.sin(t0)], 1),
            np.concatenate([-np.sin(t0), np.cos(t0)], 1),
            np.concatenate([np.cos(t1), np.sin(t1)], 1),
            np.concatenate([np.sin(t1), -np.cos(t1)], 1),
        ]
        tables.append(np.concatenate(rows, 0))
    m = 2 * np.arange(4)[:, None] + 1
    turn = np.pi * (m * n) / 2048
    twiddle = np.concatenate([np.cos(turn), np.sin(turn)], 0) / math.sqrt(NT)
    return np.stack(tables).astype(np.float32), twiddle.astype(np.float32)


def half_turn_fit(odd, terms):
    nodes = 0.25 * (np.cos(np.pi * (np.arange(400) + 0.5) / 400) + 1) / 2
    r = np.sqrt(nodes)
    want = np.sin(np.pi * r) / r if odd else np.cos(np.pi * r)
    fit = np.polynomial.chebyshev.Chebyshev.fit(nodes, want, terms - 1, domain=[0, 0.25])
    return [float(v) for v in fit.convert(kind=np.polynomial.Polynomial).coef]


SIN_FIT = half_turn_fit(True, 6)
COS_FIT = half_turn_fit(False, 6)


def horner(x, coef):
    total = coef[-1] * x + coef[-2]
    for value in coef[-3::-1]:
        total = total * x + value
    return total


def far_first(n):
    return sorted(range(n), key=lambda d: -min(d, n - d))


def wrap(value, n):
    return jnp.where(value >= n, value - n, value)


def kernel(raw_hbm, slot_hbm, offs_hbm, slow_hbm, twid_hbm, table_hbm, out,
           raw, slot, offs, slow, twid, table, send_a, recv_a, spec, wide,
           send_p, recv_p, send_r, recv_r, send_s, recv_s, send_t, recv_t, places, weights, spectra, curve, sums, send_d, recv_d,
           ssems, rsems, load_sems, plane_sem):
    me_k = lax.axis_index("freq")
    me_o = lax.axis_index("offset")
    me_x, me_z = me_o // NZ, me_o % NZ
    me_y = me_k // 2
    me_c = me_k - 2 * me_y

    turns_k = far_first(NK)
    peers_k = [wrap(me_k + d, NK) for d in turns_k if d]
    peers_z = {d: wrap(me_z + d, NZ) for d in range(NZ)}
    peers_x = {d: wrap(me_x + d, NX) * NZ for d in range(NX)}
    peers_o = [
        peers_x[dx] + peers_z[dz]
        for dz in far_first(NZ) for dx in far_first(NX) if dx or dz
    ]

    loads = [
        pltpu.make_async_copy(src, dst, load_sems.at[i])
        for i, (src, dst) in enumerate([
            (slot_hbm, slot), (raw_hbm, raw), (offs_hbm, offs), (slow_hbm, slow),
            (twid_hbm, twid), (table_hbm.at[me_c], table)])
    ]
    barrier = pltpu.get_barrier_semaphore()
    loads[0].start()
    loads[1].start()

    for there in peers_k:
        pl.semaphore_signal(barrier, inc=1, device_id=(there, me_o), device_id_type=MESH)
    line_z = [me_x * NZ + peers_z[d] for d in far_first(NZ) if d]
    line_x = [peers_x[d] + me_z for d in far_first(NX) if d]
    for there in line_z + line_x:
        pl.semaphore_signal(barrier, inc=1, device_id=(me_k, there), device_id_type=MESH)
    for load in loads[2:]:
        load.start()

    rings_y = [wrap(me_y + d, NY) for d in far_first(NY)]
    to_k = [((there, me_o), there) for there in peers_k]
    to_o = [((me_k, there), there) for there in peers_o]
    to_same = [((2 * there + me_c, me_o), there) for there in rings_y[:-1]]
    to_other = [((2 * there + 1 - me_c, me_o), there) for there in rings_y]
    exchanges = []

    class Exchange:
        def __init__(self, src, dst, peers, me):
            self.src, self.dst, self.peers, self.me = src, dst, peers, me
            self.ssem, self.rsem = ssems.at[len(exchanges)], rsems.at[len(exchanges)]
            exchanges.append(self)

        def send(self, device, slot):
            pltpu.make_async_remote_copy(
                src_ref=self.src.at[slot], dst_ref=self.dst.at[self.me], send_sem=self.ssem,
                recv_sem=self.rsem, device_id=device, device_id_type=MESH).start()

        def keep(self, slot):
            self.dst[self.me] = self.src[slot]

        def start(self):
            for device, slot in self.peers:
                self.send(device, slot)

        def arrive(self):
            part = self.dst.at[pl.ds(0, len(self.peers))]
            pltpu.make_async_copy(part, part, self.rsem).wait()

        def leave(self):
            part = self.src.at[pl.ds(0, len(self.peers))]
            pltpu.make_async_copy(part, part, self.ssem).wait()

    def halves(src, dst, peers, me):
        return [Exchange(src.at[h], dst.at[h], peers, me) for h in range(2)]

    ex_a = halves(send_a, recv_a, to_k, me_k)
    ex_p = halves(send_p, recv_p, to_o, me_o)
    ex_s = halves(send_s, recv_s, to_same, me_y)
    ex_r = halves(send_r, recv_r, to_other, me_y)
    ex_t = halves(send_t, recv_t, to_o, me_o)
    ex_d = Exchange(send_d, recv_d, to_o, me_o)

    loads[0].wait()
    row_ids = lax.broadcasted_iota(jnp.int32, (G, HB * G), 1)
    ahead = pltpu.roll(jnp.concatenate([slot[...]] * 4, axis=1), 4 * HB - 2 * me_k, 1)

    def choose(h, part):
        turns = turns_k[8 * part:8 * part + 8]
        return jnp.concatenate([
            jnp.where(ahead[:, 2 * d + h:2 * d + h + 1] == row_ids, 1.0, 0.0).astype(BF16)
            for d in turns
        ], axis=0)

    def pick(h, part, chosen):
        rows = jnp.dot(chosen, raw[...], preferred_element_type=F32).astype(BF16)
        send_a[h, 8 * part:8 * part + 8] = rows.reshape(8, G, 128)

    def post(h, part):
        for i in range(8 * part, 8 * part + 8):
            if turns_k[i]:
                ex_a[h].send((peers_k[i], me_o), i)
            else:
                ex_a[h].keep(i)

    chosen = choose(0, 0)
    loads[1].wait()
    pick(0, 0, chosen)
    pl.semaphore_wait(barrier, NK - 1 + NZ - 1 + NX - 1)
    post(0, 0)
    for there in line_x:
        pl.semaphore_signal(plane_sem, inc=1, device_id=(me_k, there), device_id_type=MESH)
    for h, part in [(0, 1), (1, 0), (1, 1)]:
        pick(h, part, choose(h, part))
        post(h, part)

    loads[2].wait()
    loads[3].wait()
    for half in range(2):
        row = slow[:, 128 * half:128 * half + 128].astype(F32) * CURVATURE
        curve[128 * half:128 * half + 128, :] = jnp.transpose(jnp.broadcast_to(row, (128, 128)))
    group = lax.broadcasted_iota(jnp.int32, (16, 128), 0)
    lane = lax.broadcasted_iota(jnp.int32, (16, 128), 1)
    eight = lax.broadcasted_iota(jnp.int32, (8, 128), 0)
    lane8 = lax.broadcasted_iota(jnp.int32, (8, 128), 1)
    deep = lax.broadcasted_iota(jnp.int32, (128, 128), 0)
    lane128 = lax.broadcasted_iota(jnp.int32, (128, 128), 1)
    grid = offs[...]
    digits = [(32.0, grid // 32), (1.0, grid % 32)]
    digits = [(size, digit.astype(F32).astype(BF16)) for size, digit in digits]
    place = None
    for size, digit in digits:
        for m in range(4):
            wanted = 32 * m + 2 * (2 * (group % NY) + me_c) + group // NY
            take = jnp.where(lane == wanted, 1.0, 0.0).astype(BF16)
            some = lax.dot_general(take, digit, (((1,), (1,)), ((), ())), preferred_element_type=F32)
            spread = jnp.where(lane8 % 32 == 4 * eight + m, size, 0.0).astype(BF16)
            term = jnp.dot(some.astype(BF16), spread, preferred_element_type=F32)
            place = term if place is None else place + term
    for h in range(2):
        wanted = (lane128 // 8 % 4) * 32 + 2 * (2 * (lane128 % 8) + 1 - me_c) + h
        other = None
        for size, digit in digits:
            take = jnp.where(deep == wanted, size, 0.0).astype(BF16)
            term = jnp.dot(digit, take, preferred_element_type=F32)
            other = term if other is None else other + term
        for source, base, start in [(place, NY * h, 512 * h), (other, 0, 512 * h + 256)]:
            for tile in range(2):
                at = base + 4 * tile
                row = source[at:at + 1, :]
                for i in range(1, 4):
                    row = jnp.where(lane[0:1] // 32 == i, source[at + i:at + i + 1, :], row)
                places[:, start + 128 * tile:start + 128 * tile + 128] = row
    first = 64 * me_k + 8 * me_z + me_x
    second = 64 * me_k + 8 * me_z + 7 - me_x
    rates = [(2 * f + 1).astype(F32) * (1.0 / (2 * NT)) for f in (first, second)]

    def weigh(block, c):
        steep = curve[pl.ds(pl.multiple_of(block * 16, 16), 16), :]
        base = block // 4 * 128 + block % 4 * 16
        rows = pl.ds(pl.multiple_of(base, 16), 16)
        low = pl.ds(pl.multiple_of(base + 64, 16), 16)
        for part in range(NH // 256):
            lanes = slice(256 * part, 256 * part + 256)
            spread = jnp.concatenate([steep, steep], axis=1) * places[:, lanes]
            delay = jnp.sqrt(APEX_TIME * APEX_TIME + spread * spread) - APEX_TIME
            for f in range(2):
                turns = delay * rates[f]
                r = turns - jnp.round(turns)
                r2 = r * r
                s = horner(r2, SIN_FIT) * r
                q = horner(r2, COS_FIT)
                start = part // 2 * NH + f * (NH // 2) + part % 2 * 256
                into = slice(start, start + 256)
                weights[rows, into] = (1.0 - 2.0 * (s * s)).astype(BF16)
                weights[low, into] = (2.0 * (s * q)).astype(BF16)
        return c

    lax.fori_loop(0, NP // 16, weigh, 0)
    loads[4].wait()
    loads[5].wait()

    lane = lax.broadcasted_iota(jnp.int32, (128, 128), 1) // 32

    def transform(h):
        for part in range(2):
            x = [recv_a[h, 2 * d + part].astype(F32) for d in range(8)]
            less = [x[d] - x[8 - d] for d in range(1, 4)]
            more = [x[d] + x[8 - d] for d in range(1, 4)]
            for b in range(4):
                m = 2 * b + 1
                yr = x[0]
                yi = x[4] * (-math.sin(math.pi * m / 2))
                for d in range(1, 4):
                    yr = yr + less[d - 1] * math.cos(math.pi * d * m / 8)
                    yi = yi - more[d - 1] * math.sin(math.pi * d * m / 8)
                tc = twid[b:b + 1, 128 * part:128 * part + 128]
                ts = twid[4 + b:5 + b, 128 * part:128 * part + 128]
                for half, value in enumerate([yr * tc + yi * ts, yi * tc - yr * ts]):
                    high = value.astype(BF16)
                    rest = (value - high.astype(F32)).astype(BF16)
                    lanes = slice(256 * half + 128 * part, 256 * half + 128 * part + 128)
                    spec[G * b:G * b + G, lanes] = high
                    spec[128 + G * b:128 + G * b + G, lanes] = rest
        whole = lax.dot_general(table[...], spec[...], (((1,), (1,)), ((), ())),
                                preferred_element_type=F32)
        whole = whole[:, 0:128] + whole[:, 128:256]
        parts = [whole[128 * c:128 * c + 128, :] for c in range(4)]
        bottoms = []
        for b in range(4):
            total = None
            for c in range(4):
                moved = parts[c] if c == b else pltpu.roll(parts[c], (c - b) * 32 % 128, 1)
                total = moved if c == 0 else jnp.where(lane == c, moved, total)
            send_p[h, 8 * b:8 * b + 8] = total[0:64].reshape(NZ, NY, 128).astype(BF16)
            bottoms.append(total[64:128].reshape(NY, NZ, 128))
        for t in range(2):
            pair = jnp.concatenate(bottoms[2 * t:2 * t + 2], axis=1).astype(BF16)
            send_r[h, :, 16 * t:16 * t + 16, :] = pair

    def turn_p(h):
        wide[...] = recv_p[h].astype(F32).reshape(NO * NY, 128)
        for y in range(NY):
            send_s[h, y] = wide[pl.ds(y, NO, stride=NY), :].astype(BF16)

    def turn_r(h):
        wide[...] = recv_r[h].astype(F32).reshape(NO * NY, 128)
        for o in range(NO):
            send_t[h, o] = wide[pl.ds(o, NY, stride=NO), :].astype(BF16)

    for h in range(2):
        ex_a[h].arrive()
        transform(h)
        if h == 0:
            pl.semaphore_wait(plane_sem, NX - 1)
        ex_r[h].start()
        ex_p[h].start()
        ex_p[h].keep(me_o)
    for h in range(2):
        ex_r[h].arrive()
        turn_r(h)
        ex_t[h].start()
        ex_t[h].keep(me_o)
        ex_p[h].arrive()
        turn_p(h)
        ex_s[h].start()
        ex_s[h].keep(me_y)

    def collect(h):
        for start, rows in [(0, recv_s[h].reshape(NH // 4, 128).astype(F32)),
                            (NH // 4, recv_t[h].astype(F32).reshape(NH // 4, 128))]:
            for f in range(2):
                at = start + f * (NH // 2)
                kept = (deep2 < 64) if f == 0 else (deep2 >= 64)
                spectra[at:at + NH // 4, :] = jnp.where(kept, rows, 0.0).astype(BF16)

    def merged(rows, h):
        return jnp.dot(weights[rows, NH * h:NH * h + NH], spectra[...], preferred_element_type=F32)

    deep2 = lax.broadcasted_iota(jnp.int32, (NH // 4, 128), 1)
    side = lax.broadcasted_iota(jnp.int32, (64, 128), 1)
    ex_s[0].arrive()
    ex_t[0].arrive()
    collect(0)
    for block in range(2):
        rows = slice(NP * block, NP * block + NP)
        sums[rows, :] = merged(rows, 0)
    ex_s[1].arrive()
    ex_t[1].arrive()
    collect(1)
    for dx in far_first(NX):
        rows = pl.ds(pl.multiple_of(peers_x[dx] * 16, 128), 128)
        both = sums[rows, :] + merged(rows, 1)
        ca, sa = both[0:64], both[64:128]
        swapped = jnp.where(side % 64 < 32, -pltpu.roll(sa, 96, 1), pltpu.roll(sa, 32, 1))
        panel = (ca + swapped) * (1.0 / math.sqrt(NH))
        send_d[pl.ds(peers_x[dx], 8)] = panel.reshape(8, 8, 128).astype(BF16)
        for dz in far_first(NZ):
            there = peers_x[dx] + peers_z[dz]
            if dx or dz:
                ex_d.send((me_k, there), there)
            else:
                ex_d.keep(there)
    ex_d.arrive()
    for o in range(NO):
        one = recv_d[o].astype(F32)
        f0 = 8 * (o % NZ) + o // NZ
        f1 = 8 * (o % NZ) + 7 - o // NZ
        out[pl.ds(f0, 8, stride=64), :] = one[:, 0:64]
        out[pl.ds(f1, 8, stride=64), :] = one[:, 64:128]

    for ex in exchanges:
        ex.leave()


def local(raw_traces, trace_slot, offset_index, slowness_index):
    table, twiddle = dft_tables()
    dma = pltpu.SemaphoreType.DMA
    got = pl.pallas_call(
        kernel,
        out_shape=pltpu.VMEM((8 * 64, 64), F32),
        in_specs=[pl.BlockSpec(memory_space=pltpu.HBM)] * 6,
        out_specs=pl.BlockSpec(memory_space=pltpu.VMEM),
        scratch_shapes=[
            pltpu.VMEM((HB * G, 128), BF16), pltpu.VMEM((G, HB), jnp.int32),
            pltpu.VMEM((8, 128), jnp.int32), pltpu.VMEM((1, NP), jnp.int32),
            pltpu.VMEM((8, 256), F32), pltpu.VMEM((512, 512), BF16),
            pltpu.VMEM((2, NK, G, 128), BF16), pltpu.VMEM((2, NK, G, 128), BF16),
            pltpu.VMEM((256, 512), BF16),
            pltpu.VMEM((NO * NY, 128), F32),
            pltpu.VMEM((2, NO, NY, 128), BF16), pltpu.VMEM((2, NO, NY, 128), BF16),
            pltpu.VMEM((2, NY, NO, 128), BF16), pltpu.VMEM((2, NY, NO, 128), BF16),
            pltpu.VMEM((2, NY, NO, 128), BF16), pltpu.VMEM((2, NY, NO, 128), BF16),
            pltpu.VMEM((2, NO, NY, 128), BF16), pltpu.VMEM((2, NO, NY, 128), BF16),
            pltpu.VMEM((1, NH), F32),
            pltpu.VMEM((2 * NP, 2 * NH), BF16), pltpu.VMEM((NH, 128), BF16),
            pltpu.VMEM((NP, 128), F32), pltpu.VMEM((2 * NP, 128), F32),
            pltpu.VMEM((NO, 8, 128), BF16), pltpu.VMEM((NO, 8, 128), BF16),
            dma((11,)), dma((11,)), dma((6,)), pltpu.SemaphoreType.REGULAR,
        ],
        compiler_params=pltpu.CompilerParams(collective_id=0, has_side_effects=True, vmem_limit_bytes=16 * 1024 * 1024),
        name="radon",
    )(*(pltpu.with_memory_space_constraint(v, pltpu.HBM) for v in (
        raw_traces, trace_slot, offset_index.reshape(8, 128), slowness_index.reshape(1, NP),
        jnp.asarray(twiddle), jnp.asarray(table, dtype=BF16))))
    return got.reshape(8, 64, 64)


def solution(mesh):
    placed = (P("offset", "freq"), P(None, "offset"), P(), P())
    return jax.shard_map(
        local, mesh=mesh, in_specs=placed, out_specs=P("offset", "freq", None), check_vma=False
    )
```

```python
import functools
import math

import jax
import jax.numpy as jnp
import numpy as np
from jax import lax
from jax.experimental import pallas as pl
from jax.experimental.pallas import tpu as pltpu
from jax.sharding import PartitionSpec as P

NT = 2048
NF = 1024
NP = 256
G = 32
HB = 32
NH = 1024
NK = 16
NO = 32
NX = 4
NY = 8
NZ = 8
APEX_TIME = 100.0
CURVATURE = 0.0003
MESH = pl.DeviceIdType.MESH
F32 = jnp.float32
BF16 = jnp.bfloat16


def dft_tables():
    n = np.arange(256)[None, :]
    high = np.arange(64) // 8
    low = np.arange(64) % 8
    tables = []
    for core in range(2):
        same = 8 * (2 * low + core) + high
        other = 8 * (2 * high + 1 - core) + low
        a = np.concatenate([same, other])[:, None]
        t0 = 2 * np.pi * ((a * n) % 256) / 256
        t1 = 2 * np.pi * (((255 - a) * n) % 256) / 256
        rows = [
            np.concatenate([np.cos(t0), np.sin(t0)], 1),
            np.concatenate([-np.sin(t0), np.cos(t0)], 1),
            np.concatenate([np.cos(t1), np.sin(t1)], 1),
            np.concatenate([np.sin(t1), -np.cos(t1)], 1),
        ]
        tables.append(np.concatenate(rows, 0))
    m = 2 * np.arange(4)[:, None] + 1
    turn = np.pi * (m * n) / 2048
    twiddle = np.concatenate([np.cos(turn), np.sin(turn)], 0) / math.sqrt(NT)
    return np.stack(tables).astype(np.float32), twiddle.astype(np.float32)


def half_turn_fit(odd, terms):
    nodes = 0.25 * (np.cos(np.pi * (np.arange(400) + 0.5) / 400) + 1) / 2
    r = np.sqrt(nodes)
    want = np.sin(np.pi * r) / r if odd else np.cos(np.pi * r)
    fit = np.polynomial.chebyshev.Chebyshev.fit(nodes, want, terms - 1, domain=[0, 0.25])
    return [float(v) for v in fit.convert(kind=np.polynomial.Polynomial).coef]


SIN_FIT = half_turn_fit(True, 6)
COS_FIT = half_turn_fit(False, 6)


def horner(x, coef):
    total = coef[-1] * x + coef[-2]
    for value in coef[-3::-1]:
        total = total * x + value
    return total


def far_first(n):
    return sorted(range(n), key=lambda d: -min(d, n - d))


def wrap(value, n):
    return jnp.where(value >= n, value - n, value)


def kernel(raw_hbm, slot_hbm, offs_hbm, slow_hbm, twid_hbm, table_hbm, out,
           raw, slot, offs, slow, twid, table, send_a, recv_a, spec, wide,
           send_p, recv_p, send_r, recv_r, send_s, recv_s, send_t, recv_t, places, weights, spectra, curve, sums, send_d, recv_d,
           ssems, rsems, load_sems, plane_sem):
    me_k = lax.axis_index("freq")
    me_o = lax.axis_index("offset")
    me_x, me_z = me_o // NZ, me_o % NZ
    me_y = me_k // 2
    me_c = me_k - 2 * me_y

    turns_k = far_first(NK)
    peers_k = [wrap(me_k + d, NK) for d in turns_k if d]
    peers_z = {d: wrap(me_z + d, NZ) for d in range(NZ)}
    peers_x = {d: wrap(me_x + d, NX) * NZ for d in range(NX)}
    peers_o = [
        peers_x[dx] + peers_z[dz]
        for dz in far_first(NZ) for dx in far_first(NX) if dx or dz
    ]

    loads = [
        pltpu.make_async_copy(src, dst, load_sems.at[i])
        for i, (src, dst) in enumerate([
            (slot_hbm, slot), (raw_hbm, raw), (offs_hbm, offs), (slow_hbm, slow),
            (twid_hbm, twid), (table_hbm.at[me_c], table)])
    ]
    barrier = pltpu.get_barrier_semaphore()
    loads[0].start()
    loads[1].start()

    for there in peers_k:
        pl.semaphore_signal(barrier, inc=1, device_id=(there, me_o), device_id_type=MESH)
    line_z = [me_x * NZ + peers_z[d] for d in far_first(NZ) if d]
    line_x = [peers_x[d] + me_z for d in far_first(NX) if d]
    for there in line_z + line_x:
        pl.semaphore_signal(barrier, inc=1, device_id=(me_k, there), device_id_type=MESH)
    for load in loads[2:]:
        load.start()

    rings_y = [wrap(me_y + d, NY) for d in far_first(NY)]
    to_k = [((there, me_o), there) for there in peers_k]
    to_o = [((me_k, there), there) for there in peers_o]
    to_same = [((2 * there + me_c, me_o), there) for there in rings_y[:-1]]
    to_other = [((2 * there + 1 - me_c, me_o), there) for there in rings_y]
    exchanges = []

    class Exchange:
        def __init__(self, src, dst, peers, me):
            self.src, self.dst, self.peers, self.me = src, dst, peers, me
            self.ssem, self.rsem = ssems.at[len(exchanges)], rsems.at[len(exchanges)]
            exchanges.append(self)

        def send(self, device, slot):
            pltpu.make_async_remote_copy(
                src_ref=self.src.at[slot], dst_ref=self.dst.at[self.me], send_sem=self.ssem,
                recv_sem=self.rsem, device_id=device, device_id_type=MESH).start()

        def keep(self, slot):
            self.dst[self.me] = self.src[slot]

        def start(self):
            for device, slot in self.peers:
                self.send(device, slot)

        def arrive(self):
            part = self.dst.at[pl.ds(0, len(self.peers))]
            pltpu.make_async_copy(part, part, self.rsem).wait()

        def leave(self):
            part = self.src.at[pl.ds(0, len(self.peers))]
            pltpu.make_async_copy(part, part, self.ssem).wait()

    def halves(src, dst, peers, me):
        return [Exchange(src.at[h], dst.at[h], peers, me) for h in range(2)]

    ex_a = halves(send_a, recv_a, to_k, me_k)
    ex_p = halves(send_p, recv_p, to_o, me_o)
    ex_s = halves(send_s, recv_s, to_same, me_y)
    ex_r = halves(send_r, recv_r, to_other, me_y)
    ex_t = halves(send_t, recv_t, to_o, me_o)
    ex_d = Exchange(send_d, recv_d, to_o, me_o)

    loads[0].wait()
    row_ids = lax.broadcasted_iota(jnp.int32, (G, HB * G), 1)
    ahead = pltpu.roll(jnp.concatenate([slot[...]] * 4, axis=1), 4 * HB - 2 * me_k, 1)

    def choose(h, part):
        turns = turns_k[8 * part:8 * part + 8]
        return jnp.concatenate([
            jnp.where(ahead[:, 2 * d + h:2 * d + h + 1] == row_ids, 1.0, 0.0).astype(BF16)
            for d in turns
        ], axis=0)

    def pick(h, part, chosen):
        rows = jnp.dot(chosen, raw[...], preferred_element_type=F32).astype(BF16)
        send_a[h, 8 * part:8 * part + 8] = rows.reshape(8, G, 128)

    def post(h, part):
        for i in range(8 * part, 8 * part + 8):
            if turns_k[i]:
                ex_a[h].send((peers_k[i], me_o), i)
            else:
                ex_a[h].keep(i)

    chosen = choose(0, 0)
    loads[1].wait()
    pick(0, 0, chosen)
    pl.semaphore_wait(barrier, NK - 1 + NZ - 1 + NX - 1)
    post(0, 0)
    for there in line_x:
        pl.semaphore_signal(plane_sem, inc=1, device_id=(me_k, there), device_id_type=MESH)
    for h, part in [(0, 1), (1, 0), (1, 1)]:
        pick(h, part, choose(h, part))
        post(h, part)

    loads[2].wait()
    loads[3].wait()
    for half in range(2):
        row = slow[:, 128 * half:128 * half + 128].astype(F32) * CURVATURE
        curve[128 * half:128 * half + 128, :] = jnp.transpose(jnp.broadcast_to(row, (128, 128)))
    group = lax.broadcasted_iota(jnp.int32, (16, 128), 0)
    lane = lax.broadcasted_iota(jnp.int32, (16, 128), 1)
    eight = lax.broadcasted_iota(jnp.int32, (8, 128), 0)
    lane8 = lax.broadcasted_iota(jnp.int32, (8, 128), 1)
    deep = lax.broadcasted_iota(jnp.int32, (128, 128), 0)
    lane128 = lax.broadcasted_iota(jnp.int32, (128, 128), 1)
    grid = offs[...]
    digits = [(32.0, grid // 32), (1.0, grid % 32)]
    digits = [(size, digit.astype(F32).astype(BF16)) for size, digit in digits]
    place = None
    for size, digit in digits:
        for m in range(4):
            wanted = 32 * m + 2 * (2 * (group % NY) + me_c) + group // NY
            take = jnp.where(lane == wanted, 1.0, 0.0).astype(BF16)
            some = lax.dot_general(take, digit, (((1,), (1,)), ((), ())), preferred_element_type=F32)
            spread = jnp.where(lane8 % 32 == 4 * eight + m, size, 0.0).astype(BF16)
            term = jnp.dot(some.astype(BF16), spread, preferred_element_type=F32)
            place = term if place is None else place + term
    for h in range(2):
        wanted = (lane128 // 8 % 4) * 32 + 2 * (2 * (lane128 % 8) + 1 - me_c) + h
        other = None
        for size, digit in digits:
            take = jnp.where(deep == wanted, size, 0.0).astype(BF16)
            term = jnp.dot(digit, take, preferred_element_type=F32)
            other = term if other is None else other + term
        for source, base, start in [(place, NY * h, 512 * h), (other, 0, 512 * h + 256)]:
            for tile in range(2):
                at = base + 4 * tile
                row = source[at:at + 1, :]
                for i in range(1, 4):
                    row = jnp.where(lane[0:1] // 32 == i, source[at + i:at + i + 1, :], row)
                places[:, start + 128 * tile:start + 128 * tile + 128] = row
    first = 64 * me_k + 8 * me_z + me_x
    second = 64 * me_k + 8 * me_z + 7 - me_x
    rates = [(2 * f + 1).astype(F32) * (1.0 / (2 * NT)) for f in (first, second)]

    def weigh(block, c):
        steep = curve[pl.ds(pl.multiple_of(block * 16, 16), 16), :]
        base = block // 4 * 128 + block % 4 * 16
        rows = pl.ds(pl.multiple_of(base, 16), 16)
        low = pl.ds(pl.multiple_of(base + 64, 16), 16)
        for part in range(NH // 256):
            lanes = slice(256 * part, 256 * part + 256)
            spread = jnp.concatenate([steep, steep], axis=1) * places[:, lanes]
            delay = jnp.sqrt(APEX_TIME * APEX_TIME + spread * spread) - APEX_TIME
            for f in range(2):
                turns = delay * rates[f]
                r = turns - jnp.round(turns)
                r2 = r * r
                s = horner(r2, SIN_FIT) * r
                q = horner(r2, COS_FIT)
                start = part // 2 * NH + f * (NH // 2) + part % 2 * 256
                into = slice(start, start + 256)
                weights[rows, into] = (1.0 - 2.0 * (s * s)).astype(BF16)
                weights[low, into] = (2.0 * (s * q)).astype(BF16)
        return c

    lax.fori_loop(0, NP // 16, weigh, 0)
    loads[4].wait()
    loads[5].wait()

    lane = lax.broadcasted_iota(jnp.int32, (128, 128), 1) // 32

    def transform(h):
        for part in range(2):
            x = [recv_a[h, 2 * d + part].astype(F32) for d in range(8)]
            less = [x[d] - x[8 - d] for d in range(1, 4)]
            more = [x[d] + x[8 - d] for d in range(1, 4)]
            for b in range(4):
                m = 2 * b + 1
                yr = x[0]
                yi = x[4] * (-math.sin(math.pi * m / 2))
                for d in range(1, 4):
                    yr = yr + less[d - 1] * math.cos(math.pi * d * m / 8)
                    yi = yi - more[d - 1] * math.sin(math.pi * d * m / 8)
                tc = twid[b:b + 1, 128 * part:128 * part + 128]
                ts = twid[4 + b:5 + b, 128 * part:128 * part + 128]
                for half, value in enumerate([yr * tc + yi * ts, yi * tc - yr * ts]):
                    high = value.astype(BF16)
                    rest = (value - high.astype(F32)).astype(BF16)
                    lanes = slice(256 * half + 128 * part, 256 * half + 128 * part + 128)
                    spec[G * b:G * b + G, lanes] = high
                    spec[128 + G * b:128 + G * b + G, lanes] = rest
        whole = lax.dot_general(table[...], spec[...], (((1,), (1,)), ((), ())),
                                preferred_element_type=F32)
        whole = whole[:, 0:128] + whole[:, 128:256]
        parts = [whole[128 * c:128 * c + 128, :] for c in range(4)]
        bottoms = []
        for b in range(4):
            total = None
            for c in range(4):
                moved = parts[c] if c == b else pltpu.roll(parts[c], (c - b) * 32 % 128, 1)
                total = moved if c == 0 else jnp.where(lane == c, moved, total)
            send_p[h, 8 * b:8 * b + 8] = total[0:64].reshape(NZ, NY, 128).astype(BF16)
            bottoms.append(total[64:128].reshape(NY, NZ, 128))
        for t in range(2):
            pair = jnp.concatenate(bottoms[2 * t:2 * t + 2], axis=1).astype(BF16)
            send_r[h, :, 16 * t:16 * t + 16, :] = pair

    def turn_p(h):
        wide[...] = recv_p[h].astype(F32).reshape(NO * NY, 128)
        for y in range(NY):
            send_s[h, y] = wide[pl.ds(y, NO, stride=NY), :].astype(BF16)

    def turn_r(h):
        wide[...] = recv_r[h].astype(F32).reshape(NO * NY, 128)
        for o in range(NO):
            send_t[h, o] = wide[pl.ds(o, NY, stride=NO), :].astype(BF16)

    for h in range(2):
        ex_a[h].arrive()
        transform(h)
        if h == 0:
            pl.semaphore_wait(plane_sem, NX - 1)
        ex_r[h].start()
        ex_p[h].start()
        ex_p[h].keep(me_o)
    for h in range(2):
        ex_r[h].arrive()
        turn_r(h)
        ex_t[h].start()
        ex_t[h].keep(me_o)
        ex_p[h].arrive()
        turn_p(h)
        ex_s[h].start()
        ex_s[h].keep(me_y)

    def collect(h):
        for start, rows in [(0, recv_s[h].reshape(NH // 4, 128).astype(F32)),
                            (NH // 4, recv_t[h].astype(F32).reshape(NH // 4, 128))]:
            for f in range(2):
                at = start + f * (NH // 2)
                kept = (deep2 < 64) if f == 0 else (deep2 >= 64)
                spectra[at:at + NH // 4, :] = jnp.where(kept, rows, 0.0).astype(BF16)

    def merged(rows, h):
        return jnp.dot(weights[rows, NH * h:NH * h + NH], spectra[...], preferred_element_type=F32)

    deep2 = lax.broadcasted_iota(jnp.int32, (NH // 4, 128), 1)
    side = lax.broadcasted_iota(jnp.int32, (64, 128), 1)
    ex_s[0].arrive()
    ex_t[0].arrive()
    collect(0)
    for block in range(2):
        rows = slice(NP * block, NP * block + NP)
        sums[rows, :] = merged(rows, 0)
    ex_s[1].arrive()
    ex_t[1].arrive()
    collect(1)
    for block in range(4):
        rows = slice(128 * block, 128 * block + 128)
        both = sums[rows, :] + merged(rows, 1)
        ca, sa = both[0:64], both[64:128]
        swapped = jnp.where(side % 64 < 32, -pltpu.roll(sa, 96, 1), pltpu.roll(sa, 32, 1))
        panel = (ca + swapped) * (1.0 / math.sqrt(NH))
        send_d[8 * block:8 * block + 8] = panel.reshape(8, 8, 128).astype(BF16)
    for device, slot in to_o:
        ex_d.send(device, slot)
    ex_d.keep(me_o)
    ex_d.arrive()
    for o in range(NO):
        one = recv_d[o].astype(F32)
        f0 = 8 * (o % NZ) + o // NZ
        f1 = 8 * (o % NZ) + 7 - o // NZ
        out[pl.ds(f0, 8, stride=64), :] = one[:, 0:64]
        out[pl.ds(f1, 8, stride=64), :] = one[:, 64:128]

    for ex in exchanges:
        ex.leave()


def local(raw_traces, trace_slot, offset_index, slowness_index):
    table, twiddle = dft_tables()
    dma = pltpu.SemaphoreType.DMA
    got = pl.pallas_call(
        kernel,
        out_shape=pltpu.VMEM((8 * 64, 64), F32),
        in_specs=[pl.BlockSpec(memory_space=pltpu.HBM)] * 6,
        out_specs=pl.BlockSpec(memory_space=pltpu.VMEM),
        scratch_shapes=[
            pltpu.VMEM((HB * G, 128), BF16), pltpu.VMEM((G, HB), jnp.int32),
            pltpu.VMEM((8, 128), jnp.int32), pltpu.VMEM((1, NP), jnp.int32),
            pltpu.VMEM((8, 256), F32), pltpu.VMEM((512, 512), BF16),
            pltpu.VMEM((2, NK, G, 128), BF16), pltpu.VMEM((2, NK, G, 128), BF16),
            pltpu.VMEM((256, 512), BF16),
            pltpu.VMEM((NO * NY, 128), F32),
            pltpu.VMEM((2, NO, NY, 128), BF16), pltpu.VMEM((2, NO, NY, 128), BF16),
            pltpu.VMEM((2, NY, NO, 128), BF16), pltpu.VMEM((2, NY, NO, 128), BF16),
            pltpu.VMEM((2, NY, NO, 128), BF16), pltpu.VMEM((2, NY, NO, 128), BF16),
            pltpu.VMEM((2, NO, NY, 128), BF16), pltpu.VMEM((2, NO, NY, 128), BF16),
            pltpu.VMEM((1, NH), F32),
            pltpu.VMEM((2 * NP, 2 * NH), BF16), pltpu.VMEM((NH, 128), BF16),
            pltpu.VMEM((NP, 128), F32), pltpu.VMEM((2 * NP, 128), F32),
            pltpu.VMEM((NO, 8, 128), BF16), pltpu.VMEM((NO, 8, 128), BF16),
            dma((11,)), dma((11,)), dma((6,)), pltpu.SemaphoreType.REGULAR,
        ],
        compiler_params=pltpu.CompilerParams(collective_id=0, has_side_effects=True, vmem_limit_bytes=16 * 1024 * 1024),
        name="radon",
    )(*(pltpu.with_memory_space_constraint(v, pltpu.HBM) for v in (
        raw_traces, trace_slot, offset_index.reshape(8, 128), slowness_index.reshape(1, NP),
        jnp.asarray(twiddle), jnp.asarray(table, dtype=BF16))))
    return got.reshape(8, 64, 64)


def solution(mesh):
    placed = (P("offset", "freq"), P(None, "offset"), P(), P())
    return jax.shard_map(
        local, mesh=mesh, in_specs=placed, out_specs=P("offset", "freq", None), check_vma=False
    )
```

```python
import functools
import math

import jax
import jax.numpy as jnp
import numpy as np
from jax import lax
from jax.experimental import pallas as pl
from jax.experimental.pallas import tpu as pltpu
from jax.sharding import PartitionSpec as P

NT = 2048
NF = 1024
NP = 256
G = 32
HB = 32
NH = 1024
NK = 16
NO = 32
NX = 4
NY = 8
NZ = 8
APEX_TIME = 100.0
CURVATURE = 0.0003
MESH = pl.DeviceIdType.MESH
F32 = jnp.float32
BF16 = jnp.bfloat16


def dft_tables():
    n = np.arange(256)[None, :]
    high = np.arange(64) // 8
    low = np.arange(64) % 8
    tables = []
    for core in range(2):
        same = 8 * (2 * low + core) + high
        other = 8 * (2 * high + 1 - core) + low
        a = np.concatenate([same, other])[:, None]
        t0 = 2 * np.pi * ((a * n) % 256) / 256
        t1 = 2 * np.pi * (((255 - a) * n) % 256) / 256
        rows = [
            np.concatenate([np.cos(t0), np.sin(t0)], 1),
            np.concatenate([-np.sin(t0), np.cos(t0)], 1),
            np.concatenate([np.cos(t1), np.sin(t1)], 1),
            np.concatenate([np.sin(t1), -np.cos(t1)], 1),
        ]
        tables.append(np.concatenate(rows, 0))
    m = 2 * np.arange(4)[:, None] + 1
    turn = np.pi * (m * n) / 2048
    twiddle = np.concatenate([np.cos(turn), np.sin(turn)], 0) / math.sqrt(NT)
    return np.stack(tables).astype(np.float32), twiddle.astype(np.float32)


def half_turn_fit(odd, terms):
    nodes = 0.25 * (np.cos(np.pi * (np.arange(400) + 0.5) / 400) + 1) / 2
    r = np.sqrt(nodes)
    want = np.sin(np.pi * r) / r if odd else np.cos(np.pi * r)
    fit = np.polynomial.chebyshev.Chebyshev.fit(nodes, want, terms - 1, domain=[0, 0.25])
    return [float(v) for v in fit.convert(kind=np.polynomial.Polynomial).coef]


SIN_FIT = half_turn_fit(True, 6)
COS_FIT = half_turn_fit(False, 6)


def horner(x, coef):
    total = coef[-1] * x + coef[-2]
    for value in coef[-3::-1]:
        total = total * x + value
    return total


def far_first(n):
    return sorted(range(n), key=lambda d: -min(d, n - d))


def wrap(value, n):
    return jnp.where(value >= n, value - n, value)


def kernel(raw_hbm, slot_hbm, offs_hbm, slow_hbm, twid_hbm, table_hbm, out,
           raw, slot, offs, slow, twid, table, send_a, recv_a, spec, wide,
           send_p, recv_p, send_r, recv_r, send_s, recv_s, send_t, recv_t, places, weights, spectra, curve, sums, send_d, recv_d,
           ssems, rsems, load_sems, plane_sem):
    me_k = lax.axis_index("freq")
    me_o = lax.axis_index("offset")
    me_x, me_z = me_o // NZ, me_o % NZ
    me_y = me_k // 2
    me_c = me_k - 2 * me_y

    turns_k = far_first(NK)
    peers_k = [wrap(me_k + d, NK) for d in turns_k if d]
    peers_z = {d: wrap(me_z + d, NZ) for d in range(NZ)}
    peers_x = {d: wrap(me_x + d, NX) * NZ for d in range(NX)}
    hops = sorted(
        [(dx, dz) for dz in far_first(NZ) for dx in far_first(NX) if dx or dz],
        key=lambda d: -min(d[0], NX - d[0]) - min(d[1], NZ - d[1]))
    peers_o = [peers_x[dx] + peers_z[dz] for dx, dz in hops]

    loads = [
        pltpu.make_async_copy(src, dst, load_sems.at[i])
        for i, (src, dst) in enumerate([
            (slot_hbm, slot), (raw_hbm, raw), (offs_hbm, offs), (slow_hbm, slow),
            (twid_hbm, twid), (table_hbm.at[me_c], table)])
    ]
    barrier = pltpu.get_barrier_semaphore()
    loads[0].start()
    loads[1].start()

    for there in peers_k:
        pl.semaphore_signal(barrier, inc=1, device_id=(there, me_o), device_id_type=MESH)
    line_z = [me_x * NZ + peers_z[d] for d in far_first(NZ) if d]
    line_x = [peers_x[d] + me_z for d in far_first(NX) if d]
    for there in line_z + line_x:
        pl.semaphore_signal(barrier, inc=1, device_id=(me_k, there), device_id_type=MESH)
    for load in loads[2:]:
        load.start()

    rings_y = [wrap(me_y + d, NY) for d in far_first(NY)]
    to_k = [((there, me_o), there) for there in peers_k]
    to_o = [((me_k, there), there) for there in peers_o]
    to_same = [((2 * there + me_c, me_o), there) for there in rings_y[:-1]]
    to_other = [((2 * there + 1 - me_c, me_o), there) for there in rings_y]
    exchanges = []

    class Exchange:
        def __init__(self, src, dst, peers, me):
            self.src, self.dst, self.peers, self.me = src, dst, peers, me
            self.ssem, self.rsem = ssems.at[len(exchanges)], rsems.at[len(exchanges)]
            exchanges.append(self)

        def send(self, device, slot):
            pltpu.make_async_remote_copy(
                src_ref=self.src.at[slot], dst_ref=self.dst.at[self.me], send_sem=self.ssem,
                recv_sem=self.rsem, device_id=device, device_id_type=MESH).start()

        def keep(self, slot):
            self.dst[self.me] = self.src[slot]

        def start(self):
            for device, slot in self.peers:
                self.send(device, slot)

        def arrive(self):
            part = self.dst.at[pl.ds(0, len(self.peers))]
            pltpu.make_async_copy(part, part, self.rsem).wait()

        def leave(self):
            part = self.src.at[pl.ds(0, len(self.peers))]
            pltpu.make_async_copy(part, part, self.ssem).wait()

    def halves(src, dst, peers, me):
        return [Exchange(src.at[h], dst.at[h], peers, me) for h in range(2)]

    ex_a = halves(send_a, recv_a, to_k, me_k)
    ex_p = halves(send_p, recv_p, to_o, me_o)
    ex_s = halves(send_s, recv_s, to_same, me_y)
    ex_r = halves(send_r, recv_r, to_other, me_y)
    ex_t = halves(send_t, recv_t, to_o, me_o)
    ex_d = Exchange(send_d, recv_d, to_o, me_o)

    loads[0].wait()
    row_ids = lax.broadcasted_iota(jnp.int32, (G, HB * G), 1)
    ahead = pltpu.roll(jnp.concatenate([slot[...]] * 4, axis=1), 4 * HB - 2 * me_k, 1)

    def choose(h, part):
        turns = turns_k[8 * part:8 * part + 8]
        return jnp.concatenate([
            jnp.where(ahead[:, 2 * d + h:2 * d + h + 1] == row_ids, 1.0, 0.0).astype(BF16)
            for d in turns
        ], axis=0)

    def pick(h, part, chosen):
        rows = jnp.dot(chosen, raw[...], preferred_element_type=F32).astype(BF16)
        send_a[h, 8 * part:8 * part + 8] = rows.reshape(8, G, 128)

    def post(h, part):
        for i in range(8 * part, 8 * part + 8):
            if turns_k[i]:
                ex_a[h].send((peers_k[i], me_o), i)
            else:
                ex_a[h].keep(i)

    chosen = choose(0, 0)
    loads[1].wait()
    pick(0, 0, chosen)
    pl.semaphore_wait(barrier, NK - 1 + NZ - 1 + NX - 1)
    post(0, 0)
    for there in line_x:
        pl.semaphore_signal(plane_sem, inc=1, device_id=(me_k, there), device_id_type=MESH)
    for h, part in [(0, 1), (1, 0), (1, 1)]:
        pick(h, part, choose(h, part))
        post(h, part)

    loads[2].wait()
    loads[3].wait()
    for half in range(2):
        row = slow[:, 128 * half:128 * half + 128].astype(F32) * CURVATURE
        curve[128 * half:128 * half + 128, :] = jnp.transpose(jnp.broadcast_to(row, (128, 128)))
    group = lax.broadcasted_iota(jnp.int32, (16, 128), 0)
    lane = lax.broadcasted_iota(jnp.int32, (16, 128), 1)
    eight = lax.broadcasted_iota(jnp.int32, (8, 128), 0)
    lane8 = lax.broadcasted_iota(jnp.int32, (8, 128), 1)
    deep = lax.broadcasted_iota(jnp.int32, (128, 128), 0)
    lane128 = lax.broadcasted_iota(jnp.int32, (128, 128), 1)
    grid = offs[...]
    digits = [(32.0, grid // 32), (1.0, grid % 32)]
    digits = [(size, digit.astype(F32).astype(BF16)) for size, digit in digits]
    place = None
    for size, digit in digits:
        for m in range(4):
            wanted = 32 * m + 2 * (2 * (group % NY) + me_c) + group // NY
            take = jnp.where(lane == wanted, 1.0, 0.0).astype(BF16)
            some = lax.dot_general(take, digit, (((1,), (1,)), ((), ())), preferred_element_type=F32)
            spread = jnp.where(lane8 % 32 == 4 * eight + m, size, 0.0).astype(BF16)
            term = jnp.dot(some.astype(BF16), spread, preferred_element_type=F32)
            place = term if place is None else place + term
    for h in range(2):
        wanted = (lane128 // 8 % 4) * 32 + 2 * (2 * (lane128 % 8) + 1 - me_c) + h
        other = None
        for size, digit in digits:
            take = jnp.where(deep == wanted, size, 0.0).astype(BF16)
            term = jnp.dot(digit, take, preferred_element_type=F32)
            other = term if other is None else other + term
        for source, base, start in [(place, NY * h, 512 * h), (other, 0, 512 * h + 256)]:
            for tile in range(2):
                at = base + 4 * tile
                row = source[at:at + 1, :]
                for i in range(1, 4):
                    row = jnp.where(lane[0:1] // 32 == i, source[at + i:at + i + 1, :], row)
                places[:, start + 128 * tile:start + 128 * tile + 128] = row
    first = 64 * me_k + 8 * me_z + me_x
    second = 64 * me_k + 8 * me_z + 7 - me_x
    rates = [(2 * f + 1).astype(F32) * (1.0 / (2 * NT)) for f in (first, second)]

    def weigh(block, c):
        steep = curve[pl.ds(pl.multiple_of(block * 16, 16), 16), :]
        base = block // 4 * 128 + block % 4 * 16
        rows = pl.ds(pl.multiple_of(base, 16), 16)
        low = pl.ds(pl.multiple_of(base + 64, 16), 16)
        for part in range(NH // 256):
            lanes = slice(256 * part, 256 * part + 256)
            spread = jnp.concatenate([steep, steep], axis=1) * places[:, lanes]
            delay = jnp.sqrt(APEX_TIME * APEX_TIME + spread * spread) - APEX_TIME
            for f in range(2):
                turns = delay * rates[f]
                r = turns - jnp.round(turns)
                r2 = r * r
                s = horner(r2, SIN_FIT) * r
                q = horner(r2, COS_FIT)
                start = part // 2 * NH + f * (NH // 2) + part % 2 * 256
                into = slice(start, start + 256)
                weights[rows, into] = (1.0 - 2.0 * (s * s)).astype(BF16)
                weights[low, into] = (2.0 * (s * q)).astype(BF16)
        return c

    lax.fori_loop(0, NP // 16, weigh, 0)
    loads[4].wait()
    loads[5].wait()

    lane = lax.broadcasted_iota(jnp.int32, (128, 128), 1) // 32

    def transform(h):
        for part in range(2):
            x = [recv_a[h, 2 * d + part].astype(F32) for d in range(8)]
            less = [x[d] - x[8 - d] for d in range(1, 4)]
            more = [x[d] + x[8 - d] for d in range(1, 4)]
            for b in range(4):
                m = 2 * b + 1
                yr = x[0]
                yi = x[4] * (-math.sin(math.pi * m / 2))
                for d in range(1, 4):
                    yr = yr + less[d - 1] * math.cos(math.pi * d * m / 8)
                    yi = yi - more[d - 1] * math.sin(math.pi * d * m / 8)
                tc = twid[b:b + 1, 128 * part:128 * part + 128]
                ts = twid[4 + b:5 + b, 128 * part:128 * part + 128]
                for half, value in enumerate([yr * tc + yi * ts, yi * tc - yr * ts]):
                    high = value.astype(BF16)
                    rest = (value - high.astype(F32)).astype(BF16)
                    lanes = slice(256 * half + 128 * part, 256 * half + 128 * part + 128)
                    spec[G * b:G * b + G, lanes] = high
                    spec[128 + G * b:128 + G * b + G, lanes] = rest
        whole = lax.dot_general(table[...], spec[...], (((1,), (1,)), ((), ())),
                                preferred_element_type=F32)
        whole = whole[:, 0:128] + whole[:, 128:256]
        parts = [whole[128 * c:128 * c + 128, :] for c in range(4)]
        bottoms = []
        for b in range(4):
            total = None
            for c in range(4):
                moved = parts[c] if c == b else pltpu.roll(parts[c], (c - b) * 32 % 128, 1)
                total = moved if c == 0 else jnp.where(lane == c, moved, total)
            send_p[h, 8 * b:8 * b + 8] = total[0:64].reshape(NZ, NY, 128).astype(BF16)
            bottoms.append(total[64:128].reshape(NY, NZ, 128))
        for t in range(2):
            pair = jnp.concatenate(bottoms[2 * t:2 * t + 2], axis=1).astype(BF16)
            send_r[h, :, 16 * t:16 * t + 16, :] = pair

    def turn_p(h):
        wide[...] = recv_p[h].astype(F32).reshape(NO * NY, 128)
        for y in range(NY):
            send_s[h, y] = wide[pl.ds(y, NO, stride=NY), :].astype(BF16)

    def turn_r(h):
        wide[...] = recv_r[h].astype(F32).reshape(NO * NY, 128)
        for o in range(NO):
            send_t[h, o] = wide[pl.ds(o, NY, stride=NO), :].astype(BF16)

    for h in range(2):
        ex_a[h].arrive()
        transform(h)
        if h == 0:
            pl.semaphore_wait(plane_sem, NX - 1)
        ex_r[h].start()
        ex_p[h].start()
        ex_p[h].keep(me_o)
    for h in range(2):
        ex_r[h].arrive()
        turn_r(h)
        ex_t[h].start()
        ex_t[h].keep(me_o)
        ex_p[h].arrive()
        turn_p(h)
        ex_s[h].start()
        ex_s[h].keep(me_y)

    def collect(h):
        for start, rows in [(0, recv_s[h].reshape(NH // 4, 128).astype(F32)),
                            (NH // 4, recv_t[h].astype(F32).reshape(NH // 4, 128))]:
            for f in range(2):
                at = start + f * (NH // 2)
                kept = (deep2 < 64) if f == 0 else (deep2 >= 64)
                spectra[at:at + NH // 4, :] = jnp.where(kept, rows, 0.0).astype(BF16)

    def merged(rows, h):
        return jnp.dot(weights[rows, NH * h:NH * h + NH], spectra[...], preferred_element_type=F32)

    deep2 = lax.broadcasted_iota(jnp.int32, (NH // 4, 128), 1)
    side = lax.broadcasted_iota(jnp.int32, (64, 128), 1)
    ex_s[0].arrive()
    ex_t[0].arrive()
    collect(0)
    for block in range(2):
        rows = slice(NP * block, NP * block + NP)
        sums[rows, :] = merged(rows, 0)
    ex_s[1].arrive()
    ex_t[1].arrive()
    collect(1)
    for block in range(4):
        rows = slice(128 * block, 128 * block + 128)
        both = sums[rows, :] + merged(rows, 1)
        ca, sa = both[0:64], both[64:128]
        swapped = jnp.where(side % 64 < 32, -pltpu.roll(sa, 96, 1), pltpu.roll(sa, 32, 1))
        panel = (ca + swapped) * (1.0 / math.sqrt(NH))
        send_d[8 * block:8 * block + 8] = panel.reshape(8, 8, 128).astype(BF16)
    for device, slot in to_o:
        ex_d.send(device, slot)
    ex_d.keep(me_o)
    ex_d.arrive()
    for o in range(NO):
        one = recv_d[o].astype(F32)
        f0 = 8 * (o % NZ) + o // NZ
        f1 = 8 * (o % NZ) + 7 - o // NZ
        out[pl.ds(f0, 8, stride=64), :] = one[:, 0:64]
        out[pl.ds(f1, 8, stride=64), :] = one[:, 64:128]

    for ex in exchanges:
        ex.leave()


def local(raw_traces, trace_slot, offset_index, slowness_index):
    table, twiddle = dft_tables()
    dma = pltpu.SemaphoreType.DMA
    got = pl.pallas_call(
        kernel,
        out_shape=pltpu.VMEM((8 * 64, 64), F32),
        in_specs=[pl.BlockSpec(memory_space=pltpu.HBM)] * 6,
        out_specs=pl.BlockSpec(memory_space=pltpu.VMEM),
        scratch_shapes=[
            pltpu.VMEM((HB * G, 128), BF16), pltpu.VMEM((G, HB), jnp.int32),
            pltpu.VMEM((8, 128), jnp.int32), pltpu.VMEM((1, NP), jnp.int32),
            pltpu.VMEM((8, 256), F32), pltpu.VMEM((512, 512), BF16),
            pltpu.VMEM((2, NK, G, 128), BF16), pltpu.VMEM((2, NK, G, 128), BF16),
            pltpu.VMEM((256, 512), BF16),
            pltpu.VMEM((NO * NY, 128), F32),
            pltpu.VMEM((2, NO, NY, 128), BF16), pltpu.VMEM((2, NO, NY, 128), BF16),
            pltpu.VMEM((2, NY, NO, 128), BF16), pltpu.VMEM((2, NY, NO, 128), BF16),
            pltpu.VMEM((2, NY, NO, 128), BF16), pltpu.VMEM((2, NY, NO, 128), BF16),
            pltpu.VMEM((2, NO, NY, 128), BF16), pltpu.VMEM((2, NO, NY, 128), BF16),
            pltpu.VMEM((1, NH), F32),
            pltpu.VMEM((2 * NP, 2 * NH), BF16), pltpu.VMEM((NH, 128), BF16),
            pltpu.VMEM((NP, 128), F32), pltpu.VMEM((2 * NP, 128), F32),
            pltpu.VMEM((NO, 8, 128), BF16), pltpu.VMEM((NO, 8, 128), BF16),
            dma((11,)), dma((11,)), dma((6,)), pltpu.SemaphoreType.REGULAR,
        ],
        compiler_params=pltpu.CompilerParams(collective_id=0, has_side_effects=True, vmem_limit_bytes=16 * 1024 * 1024),
        name="radon",
    )(*(pltpu.with_memory_space_constraint(v, pltpu.HBM) for v in (
        raw_traces, trace_slot, offset_index.reshape(8, 128), slowness_index.reshape(1, NP),
        jnp.asarray(twiddle), jnp.asarray(table, dtype=BF16))))
    return got.reshape(8, 64, 64)


def solution(mesh):
    placed = (P("offset", "freq"), P(None, "offset"), P(), P())
    return jax.shard_map(
        local, mesh=mesh, in_specs=placed, out_specs=P("offset", "freq", None), check_vma=False
    )
```
